32 devices in a mesh: dp: 2 (over y), expert: 16 (over z, x, core).
Axes of the slice: x: 2, y: 2, z: 4, core: 2. Of those that a mesh axis runs over, the one named last changes fastest.
Arguments:
- tokens: bfloat16 [4096, 2048], P(('dp', 'expert')), may hold values from -6 to 6
- cotangent: bfloat16 [4096, 2048], P(('dp', 'expert')), may hold values from -6 to 6
- gate_probs: float32 [4096, 2], P(('dp', 'expert')), may hold values from 0.2 to 1
- expert_ids: int32 [4096, 2], P(('dp', 'expert')), may hold values from 0 to 15, as said below
- route_slots: int32 [4096, 2], P(('dp', 'expert')), may hold values from 0 to 4, as said below
- hot_mask: int32 [16], replicated, may hold values from 0 to 1, as said below
- w_up: bfloat16 [16, 2048, 4096], P('expert', None, 'dp'), may hold values from -0.125 to 0.125
- w_down: bfloat16 [16, 4096, 2048], P('expert', 'dp'), may hold values from -0.09375 to 0.09375
Outputs:
- layer_out: bfloat16 [4096, 2048], P(('dp', 'expert'))
- grad_tokens: bfloat16 [4096, 2048], P(('dp', 'expert'))
- grad_up: bfloat16 [16, 2048, 4096], P(None, 'expert', 'dp')
- grad_down: bfloat16 [16, 2048, 4096], P(None, 'expert', 'dp')
The draws below stay inside these ranges and needn't reach their ends.
Inputs may be any that keep to these rules, and one draw needn't show every extreme that they name: `expert_ids`: A token's two experts differ. Only first choices name the hot expert. Every device's 128 tokens (aligned blocks) name the hot expert at least 4 + 1 times. route_slots[t, c] is the rank of route (t, c) among the routes of the same device's 128 tokens (aligned blocks) to the same expert, counting all first choices in token order before all second choices, capped at 4. `hot_mask`: exactly one entry is 1.
All inputs are finite; a program needn't handle non-finite values.
Results may differ from the reference program's by a relative error of at most 0.014.
Values may be sent and summed in bfloat16 or wider, within the bound.
No kernel may reach another device: no remote copies, remote signals or barrier semaphores. Data moves between devices by JAX's collectives and lax.ppermute only.
A program may use at most 128 MiB of HBM per device.

```python
import jax
import jax.numpy as jnp
from jax import lax

D = 2048
FF = 4096
TOK_DEV = 128
CAP = 2
HCAP = 4
EXPERTS = 16
TOKENS = 4096
N_DP = 2
N_EXPERT = 16


def route_plan(key):
    base = jax.random.fold_in(key, 11)
    key_hot, key_busy, key_order, key_first, key_second = jax.random.split(base, 5)
    blocks = N_DP * N_EXPERT
    hot_expert = jax.random.randint(key_hot, (), 0, EXPERTS)
    busy = (hot_expert + jax.random.randint(key_busy, (N_DP,), 1, EXPERTS)) % EXPERTS
    busy_block = jnp.repeat(busy, N_EXPERT)
    block_keys = jax.random.split(key_order, blocks)
    position_rank = jax.vmap(lambda one_key: jax.random.permutation(one_key, TOK_DEV))(block_keys)
    first_free = jax.random.randint(key_first, (blocks, TOK_DEV), 0, EXPERTS)
    first_pick = jnp.where(position_rank <= CAP, busy_block[:, None], jnp.where(position_rank <= CAP + HCAP + 1, hot_expert, first_free))
    offsets = jax.random.randint(key_second, (blocks, TOK_DEV), 1, EXPERTS - 1)
    second_pick = (hot_expert + offsets) % EXPERTS
    second_pick = jnp.where(second_pick == first_pick, (hot_expert + EXPERTS - 1) % EXPERTS, second_pick)
    expert_table = jnp.stack([first_pick, second_pick], axis=-1).reshape(TOKENS, 2)
    ordered = jnp.concatenate([first_pick, second_pick], axis=1)
    onehot = (ordered[:, :, None] == jnp.arange(EXPERTS)[None, None, :]).astype(jnp.int32)
    earlier = jnp.cumsum(onehot, axis=1) - onehot
    ranks = jnp.minimum(jnp.sum(earlier * onehot, axis=2), HCAP)
    slot_table = jnp.stack([ranks[:, :TOK_DEV], ranks[:, TOK_DEV:]], axis=-1).reshape(TOKENS, 2)
    mask_table = (jnp.arange(EXPERTS) == hot_expert).astype(jnp.int32)
    return (expert_table.astype(jnp.int32), slot_table.astype(jnp.int32), mask_table)


def draw_expert_ids(key, part):
    return route_plan(key)[0]


def draw_route_slots(key, part):
    return route_plan(key)[1]


def draw_hot_mask(key, part):
    return route_plan(key)[2]


def block_scale(stream_key, shape, shards, least, top_value):
    factor_of = 1.0
    for dim, blocks in shards:
        steps = jax.random.uniform(jax.random.fold_in(jax.random.fold_in(stream_key, 6), dim), (blocks,), jnp.float32, least / len(shards), top_value / len(shards))
        factor_of = factor_of * jnp.repeat(jnp.exp(steps), shape[dim] // blocks).reshape((-1,) + (1,) * (len(shape) - 1 - dim))
    return factor_of


def gaussian(own_key, dims, width, bound, pieces=(), held_as=jnp.bfloat16):
    drawn = width * jax.random.normal(own_key, dims, jnp.float32)
    if pieces:
        drawn = drawn * block_scale(own_key, dims, pieces, -0.22, 0.18)
    return jnp.clip(drawn, -bound, bound).astype(held_as)


def setup_inputs(seed: int = 0) -> dict:
    keys = jax.random.split(jax.random.key(seed), 9)
    tokens = gaussian(keys[0], (TOKENS, D), 1.0, 6.0, ((0, 32),))
    cotangent = gaussian(keys[1], (TOKENS, D), 1.0, 6.0, ((0, 32),))
    gate_probs = jnp.clip(0.2 + 0.8 * jax.random.uniform(keys[2], (TOKENS, 2), jnp.float32) ** block_scale(keys[2], (TOKENS, 2), ((0, 32),), -0.2, 0.2), 0.2, 1.0)
    expert_ids = draw_expert_ids(jax.random.fold_in(keys[8], 71), 0)
    route_slots = draw_route_slots(jax.random.fold_in(keys[8], 71), 0)
    hot_mask = draw_hot_mask(jax.random.fold_in(keys[8], 71), 0)
    w_up = gaussian(keys[6], (EXPERTS, D, FF), D ** -0.5, 0.125, ((0, 16), (2, 2)))
    w_down = gaussian(keys[7], (EXPERTS, FF, D), FF ** -0.5, 0.09375, ((0, 16), (1, 2)))
    return {"tokens": tokens, "cotangent": cotangent, "gate_probs": gate_probs, "expert_ids": expert_ids, "route_slots": route_slots, "hot_mask": hot_mask, "w_up": w_up, "w_down": w_down}


def gelu_pair(preact):
    normal_cdf = 0.5 * (1.0 + lax.erf(preact * 0.7071067811865476))
    density = jnp.exp(-0.5 * preact * preact) * 0.3989422804014327
    return preact * normal_cdf, normal_cdf + preact * density


def reference(tokens, cotangent, gate_probs, expert_ids, route_slots, hot_mask, w_up, w_down):
    blocks = N_DP * N_EXPERT
    route_count = TOKENS * 2
    slice_width = FF // N_DP
    route_index = jnp.arange(route_count, dtype=jnp.int32)
    flat_expert = expert_ids.reshape(-1).astype(jnp.int32)
    flat_slot = route_slots.reshape(-1).astype(jnp.int32)
    flat_block = ((route_index // 2) // TOK_DEV).astype(jnp.int32)
    is_hot = jnp.take(hot_mask, flat_expert) > 0
    capacity = jnp.where(is_hot, HCAP, CAP).astype(jnp.int32)
    kept_route = flat_slot < capacity
    target = jnp.where(kept_route, flat_slot, HCAP).astype(jnp.int32)
    route_table = jnp.full((EXPERTS, blocks, HCAP), -1, dtype=jnp.int32)
    route_table = route_table.at[flat_expert, flat_block, target].set(route_index, mode="drop")
    routed = (gate_probs[:, :, None] * cotangent[:, None, :].astype(jnp.float32)).astype(jnp.bfloat16)
    routed = routed.reshape(route_count, D)
    tokens_rep = jnp.repeat(tokens, 2, axis=0)

    def expert_step(totals, inputs):
        table_rows, up_weight, down_weight = inputs
        rows_index = table_rows.reshape(-1).astype(jnp.int32)
        filled = rows_index >= 0
        safe_index = jnp.maximum(rows_index, 0).astype(jnp.int32)
        rows_x = jnp.where(filled[:, None], tokens_rep[safe_index], jnp.zeros((), jnp.bfloat16))
        rows_g = jnp.where(filled[:, None], routed[safe_index], jnp.zeros((), jnp.bfloat16))
        row_count = rows_x.shape[0]
        preact = jnp.dot(rows_x, up_weight, preferred_element_type=jnp.float32)
        gelu_value, gelu_slope = gelu_pair(preact)
        activation = gelu_value.astype(jnp.bfloat16)
        partials = jnp.einsum("rjf,jfd->jrd",
                              activation.reshape(row_count, N_DP, slice_width).astype(jnp.float32),
                              down_weight.reshape(N_DP, slice_width, D).astype(jnp.float32))
        rounded = lax.optimization_barrier(partials.astype(jnp.bfloat16))
        expert_out = jnp.sum(rounded.astype(jnp.float32), axis=0).astype(jnp.bfloat16)
        d_act = jnp.dot(rows_g, down_weight.T, preferred_element_type=jnp.float32)
        d_pre = (d_act * gelu_slope).astype(jnp.bfloat16)
        back_partials = jnp.einsum("rjf,djf->jrd",
                                   d_pre.reshape(row_count, N_DP, slice_width).astype(jnp.float32),
                                   up_weight.reshape(D, N_DP, slice_width).astype(jnp.float32))
        back_rounded = lax.optimization_barrier(back_partials.astype(jnp.bfloat16))
        route_back = jnp.sum(back_rounded.astype(jnp.float32), axis=0).astype(jnp.bfloat16)
        grad_in = jnp.dot(rows_x.T, d_pre, preferred_element_type=jnp.float32).astype(jnp.bfloat16)
        grad_out = jnp.dot(rows_g.T, activation, preferred_element_type=jnp.float32).astype(jnp.bfloat16)
        out_total = totals[0].at[safe_index].add(jnp.where(filled[:, None], expert_out.astype(jnp.float32), jnp.zeros((), jnp.float32)))
        back_total = totals[1].at[safe_index].add(jnp.where(filled[:, None], route_back.astype(jnp.float32), jnp.zeros((), jnp.float32)))
        return (out_total, back_total), (grad_in, grad_out)

    zero_routes = jnp.zeros((route_count, D), jnp.float32)
    totals, grads = lax.scan(expert_step, (zero_routes, zero_routes), (route_table, w_up, w_down))
    out_total, back_total = totals
    grad_up, grad_down = grads
    layer_out = jnp.sum(gate_probs[:, :, None] * out_total.reshape(TOKENS, 2, D), axis=1).astype(jnp.bfloat16)
    grad_tokens = jnp.sum(back_total.reshape(TOKENS, 2, D), axis=1).astype(jnp.bfloat16)
    return (layer_out, grad_tokens, grad_up, grad_down)
```

```python
import functools

import jax
import jax.numpy as jnp
from jax import lax
from jax.experimental import pallas as pl
from jax.experimental.pallas import tpu as pltpu
from jax.sharding import PartitionSpec as P

CAP = 2
HCAP = 4
EXTRA = HCAP - CAP
BF16 = jnp.bfloat16
F32 = jnp.float32


def gelu_pair(preact):
    normal_cdf = 0.5 * (1.0 + lax.erf(preact * 0.7071067811865476))
    density = jnp.exp(-0.5 * preact * preact) * 0.3989422804014327
    return (preact * normal_cdf, normal_cdf + preact * density)


def contract_last(left_rows, right_rows):
    return lax.dot_general(
        left_rows, right_rows, (((1,), (1,)), ((), ())), preferred_element_type=F32
    )


def matmul(left, right):
    return jnp.dot(left, right, preferred_element_type=F32)


def chip_ring(device_count):
    chips = device_count // 2
    half = chips // 2
    return [2 * i for i in range(half)] + [2 * i + 1 for i in reversed(range(chips - half))]


def ring_pairs(device_count, shift):
    ring = chip_ring(device_count)
    size = len(ring)
    return [
        (2 * ring[k] + core, 2 * ring[(k + shift) % size] + core)
        for k in range(size)
        for core in range(2)
    ]


def send(value, pairs):
    return lax.ppermute(value, "expert", pairs)


def dp_shift(value, shift):
    count = lax.axis_size("dp")
    return lax.ppermute(value, "dp", [(p, (p + shift) % count) for p in range(count)])


def gather_planes(own):
    count = lax.axis_size("dp")
    return [own] + [dp_shift(own, -shift) for shift in range(1, count)]


def sum_planes(blocks):
    count = lax.axis_size("dp")
    total = blocks[0].astype(F32)
    for shift in range(1, count):
        total = total + dp_shift(blocks[shift], shift).astype(F32)
    return total.astype(BF16)


def flip_bit(device_count, bit):
    return [(i, i ^ bit) for i in range(device_count)]


def scatter_sum(blocks):
    count = blocks.shape[0]
    width = count.bit_length() - 1
    order = list(range(min(2, width))) + list(range(width - 1, 1, -1))
    index = lax.axis_index("expert")
    kept = list(range(width))
    shape = blocks.shape[1:]
    value = blocks.reshape((2,) * width + shape)
    for bit in order:
        axis = len(kept) - 1 - kept.index(bit)
        mine = (index >> bit) & 1
        keep = lax.dynamic_index_in_dim(value, mine, axis, keepdims=False)
        give = lax.dynamic_index_in_dim(value, 1 - mine, axis, keepdims=False)
        value = keep + send(give, flip_bit(count, 1 << bit))
        kept.remove(bit)
    return value


def ring_gather(value, far_right=True):
    count = lax.axis_size("expert")
    size = count // 2
    swap = flip_bit(count, 1)
    got = {0: value}
    for sign in (1, -1):
        far = sign > 0 if far_right else sign < 0
        going = value
        for step in range(1, (size // 2 if far else (size - 1) // 2) + 1):
            going = send(going, ring_pairs(count, sign))
            got[-(size // 2) if 2 * step == size else -sign * step] = going
    return {(d, o): (send(v, swap) if o else v) for d, v in got.items() for o in range(2)}


def ring_sources(count, distance, other):
    ring = chip_ring(count)
    size = len(ring)
    where = [ring.index(chip) for chip in range(size)]
    index = lax.axis_index("expert")
    table = jnp.array(
        [2 * ring[(where[i // 2] + distance) % size] + ((i % 2) ^ other) for i in range(count)],
        dtype=jnp.int32,
    )
    return table[index]


def grad_body(group, first, ids_ref, cols_ref, *refs):
    del ids_ref
    acts = refs[:group]
    dpres = refs[group : 2 * group]
    up_ref, down_ref = refs[2 * group + (0 if first else 2) :]
    step = pl.program_id(0)
    for k in range(group):

        @pl.when(step == k)
        def _(k=k):
            width = cols_ref.shape[2] // 2
            dims = (((0,), (0,)), ((), ()))
            up = lax.dot_general(
                cols_ref[0, :, :width], dpres[k][...], dims, preferred_element_type=F32
            )
            up_ref[0] = up.astype(BF16)
            down = lax.dot_general(
                cols_ref[0, :, width:], acts[k][...], dims, preferred_element_type=F32
            )
            down_ref[0] = down.astype(BF16)


def grad_stage(ids, cols, acts, dpres, totals, out_shape):
    group = len(acts)
    first = totals is None
    rows, hidden = acts[0].shape
    count, _, width = cols.shape
    block_rows = width // 2
    whole = pl.BlockSpec((rows, hidden), lambda i, ids: (0, 0))
    anywhere = pl.BlockSpec(memory_space=pl.ANY)
    out_spec = pl.BlockSpec((1, block_rows, hidden), lambda i, ids: (ids[i], 0, 0))
    return pl.pallas_call(
        functools.partial(grad_body, group, first),
        grid_spec=pltpu.PrefetchScalarGridSpec(
            num_scalar_prefetch=1,
            grid=(group,),
            in_specs=[pl.BlockSpec((1, rows, width), lambda i, ids: (ids[i], 0, 0))]
            + [whole] * (2 * group)
            + ([] if first else [anywhere, anywhere]),
            out_specs=[out_spec, out_spec],
        ),
        out_shape=[out_shape, out_shape],
        input_output_aliases={} if first else {2 + 2 * group: 0, 3 + 2 * group: 1},
        cost_estimate=pl.CostEstimate(
            flops=4 * group * rows * block_rows * hidden,
            bytes_accessed=4 * group * (rows + block_rows) * hidden,
            transcendentals=0,
        ),
        name="grad_stage",
    )(ids, cols, *acts, *dpres, *(() if first else totals))


def hot_body(ids_ref, cols_ref, act_ref, dpre_ref, up_in, down_in, up_ref, down_ref):
    del ids_ref
    width = cols_ref.shape[1] // 2
    dims = (((0,), (0,)), ((), ()))
    up = lax.dot_general(cols_ref[:, :width], dpre_ref[...], dims, preferred_element_type=F32)
    up_ref[0] = (up_in[0].astype(F32) + up).astype(BF16)
    down = lax.dot_general(cols_ref[:, width:], act_ref[...], dims, preferred_element_type=F32)
    down_ref[0] = (down_in[0].astype(F32) + down).astype(BF16)


def grad_hot(ids, cols, act, dpre, totals):
    rows, hidden = act.shape
    width = cols.shape[1]
    block_rows = width // 2
    whole = pl.BlockSpec((rows, hidden), lambda i, ids: (0, 0))
    spec = pl.BlockSpec((1, block_rows, hidden), lambda i, ids: (ids[0], 0, 0))
    out_shape = jax.ShapeDtypeStruct(totals[0].shape, BF16)
    return pl.pallas_call(
        hot_body,
        grid_spec=pltpu.PrefetchScalarGridSpec(
            num_scalar_prefetch=1,
            grid=(1,),
            in_specs=[pl.BlockSpec((rows, width), lambda i, ids: (0, 0)), whole, whole, spec, spec],
            out_specs=[spec, spec],
        ),
        out_shape=[out_shape, out_shape],
        input_output_aliases={4: 0, 5: 1},
        name="grad_hot",
    )(ids, cols, act, dpre, *totals)


def ffn(rows_in, rows_grad, up_local, down_local):
    gelu_value, gelu_slope = gelu_pair(matmul(rows_in, up_local))
    activation = gelu_value.astype(BF16)
    d_pre = (contract_last(rows_grad, down_local) * gelu_slope).astype(BF16)
    return activation, d_pre


def ffn_parts(activation, d_pre, up_local, down_local):
    part_out = matmul(activation, down_local).astype(BF16)
    part_back = contract_last(d_pre, up_local).astype(BF16)
    return part_out, part_back


def on_device(tokens, cotangent, gate_probs, expert_ids, route_slots, hot_mask, w_up, w_down):
    count = lax.axis_size("expert")
    planes = lax.axis_size("dp")
    index = lax.axis_index("expert")
    model_width = tokens.shape[1]
    up_local = w_up[0]
    down_local = w_down[0]
    hidden = up_local.shape[1]
    block_rows = model_width // count
    buffers = count * CAP
    codes = jnp.arange(count, dtype=jnp.int32)
    hot_index = jnp.sum(hot_mask * codes).astype(jnp.int32)
    is_owner = hot_index == index

    hot_extra = jnp.logical_and(expert_ids == hot_index, route_slots < HCAP)
    place = jnp.where(
        route_slots < CAP,
        expert_ids * CAP + route_slots,
        jnp.where(hot_extra, buffers + route_slots - CAP, -1),
    )
    slot_codes = jnp.arange(buffers + EXTRA, dtype=jnp.int32)
    picks = place[:, :, None] == slot_codes
    pick_first, pick_second = picks[:, 0].astype(BF16), picks[:, 1].astype(BF16)
    pick = pick_first + pick_second
    gate_rows = jnp.sum(jnp.where(picks, gate_probs[:, :, None], 0.0), axis=(0, 1))
    take = (((0,), (0,)), ((), ()))
    rows_x = lax.dot_general(pick, tokens, take, preferred_element_type=F32).astype(BF16)
    rows_g = (
        gate_rows[:, None] * lax.dot_general(pick, cotangent, take, preferred_element_type=F32)
    ).astype(BF16)

    def exchange(value):
        return lax.all_to_all(value, "expert", split_axis=0, concat_axis=0, tiled=True)

    arrived_x = exchange(rows_x[:buffers].reshape(count, CAP, model_width))
    flat_x = jnp.concatenate(gather_planes(arrived_x)).reshape(-1, model_width)
    arrived_g = exchange(rows_g[:buffers].reshape(count, CAP, model_width))
    flat_g = jnp.concatenate(gather_planes(arrived_g)).reshape(-1, model_width)
    activation, d_pre = ffn(flat_x, flat_g, up_local, down_local)

    acts = ring_gather(activation)
    dpres = ring_gather(d_pre, far_right=False)

    extra = jnp.concatenate([rows_x[buffers:], rows_g[buffers:]], axis=1)
    arrived_h = exchange(jnp.broadcast_to(extra[None], (count,) + extra.shape))
    arrived_h = jnp.where(is_owner, arrived_h, jnp.zeros_like(arrived_h))
    flat_h = jnp.concatenate(gather_planes(arrived_h)).reshape(-1, 2 * model_width)
    hot_act, hot_dpre = ffn(
        flat_h[:, :model_width], flat_h[:, model_width:], up_local, down_local
    )

    both = jnp.stack(
        [rows_x.reshape(-1, count, block_rows), rows_g.reshape(-1, count, block_rows)], axis=2
    )
    columns = exchange(jnp.transpose(both, (1, 0, 2, 3)).reshape(count, -1, 2 * block_rows))
    columns = jnp.stack(gather_planes(columns))
    cols = columns[:, :, :buffers].reshape(planes, count, count, CAP, 2 * block_rows)
    cols = jnp.transpose(cols, (2, 0, 1, 3, 4)).reshape(count, -1, 2 * block_rows)
    hot_cols = columns[:, :, buffers:].reshape(-1, 2 * block_rows)

    def planes_of(part_out, part_back):
        part = jnp.concatenate([part_out, part_back], axis=1)
        part = part.reshape(planes, count, -1, 2 * model_width)
        return sum_planes([part[s] for s in range(planes)])

    returned = exchange(planes_of(*ffn_parts(activation, d_pre, up_local, down_local)))
    returned = returned.reshape(buffers, 2 * model_width)
    hot_back = planes_of(*ffn_parts(hot_act, hot_dpre, up_local, down_local))
    hot_factors = jnp.concatenate([hot_act, hot_dpre], axis=1).reshape(count, -1, 2 * model_width)
    hot_rows = scatter_sum(jnp.concatenate([hot_back, hot_factors], axis=1))
    rows_back = jnp.concatenate([returned, hot_rows[:EXTRA]])
    back_out, back_grad = rows_back[:, :model_width], rows_back[:, model_width:]
    layer_out = (
        gate_probs[:, :1] * matmul(pick_first, back_out)
        + gate_probs[:, 1:] * matmul(pick_second, back_out)
    ).astype(BF16)
    grad_tokens = matmul(pick, back_grad).astype(BF16)

    out_shape = jax.ShapeDtypeStruct((count, block_rows, hidden), BF16)
    far = count // 4
    totals = None
    for step in range(far + 1):
        distances = [0] if step == 0 else ([-step] if step == far else [-step, step])
        act_of = [acts[(d, o)] for d in distances for o in range(2)]
        dpre_of = [dpres[(d, o)] for d in distances for o in range(2)]
        ids = jnp.stack([ring_sources(count, d, o) for d in distances for o in range(2)])
        totals = grad_stage(ids, cols, act_of, dpre_of, totals, out_shape)
    pieces = ring_gather(hot_rows[EXTRA:])
    ordered = jnp.zeros((count,) + hot_rows[EXTRA:].shape, BF16)
    for (d, o), piece in pieces.items():
        ordered = lax.dynamic_update_index_in_dim(ordered, piece, ring_sources(count, d, o), 0)
    ordered = ordered.reshape(-1, 2 * hidden)
    grad_up, grad_down = grad_hot(
        hot_index[None], hot_cols, ordered[:, :hidden], ordered[:, hidden:], totals
    )
    return (layer_out, grad_tokens, grad_up, grad_down)


def solution(mesh):
    placed = (
        P(("dp", "expert"), None),
        P(("dp", "expert"), None),
        P(("dp", "expert"), None),
        P(("dp", "expert"), None),
        P(("dp", "expert"), None),
        P(),
        P("expert", None, "dp"),
        P("expert", "dp", None),
    )
    return jax.shard_map(
        on_device,
        mesh=mesh,
        in_specs=placed,
        out_specs=(
            P(("dp", "expert"), None),
            P(("dp", "expert"), None),
            P(None, "expert", "dp"),
            P(None, "expert", "dp"),
        ),
        check_vma=False,
    )
```

```python
import functools

import jax
import jax.numpy as jnp
from jax import lax
from jax.experimental import pallas as pl
from jax.experimental.pallas import tpu as pltpu
from jax.sharding import PartitionSpec as P

CAP = 2
HCAP = 4
EXTRA = HCAP - CAP
BF16 = jnp.bfloat16
F32 = jnp.float32


def gelu_pair(preact):
    normal_cdf = 0.5 * (1.0 + lax.erf(preact * 0.7071067811865476))
    density = jnp.exp(-0.5 * preact * preact) * 0.3989422804014327
    return (preact * normal_cdf, normal_cdf + preact * density)


def contract_last(left_rows, right_rows):
    return lax.dot_general(
        left_rows, right_rows, (((1,), (1,)), ((), ())), preferred_element_type=F32
    )


def matmul(left, right):
    return jnp.dot(left, right, preferred_element_type=F32)


def chip_ring(device_count):
    chips = device_count // 2
    half = chips // 2
    return [2 * i for i in range(half)] + [2 * i + 1 for i in reversed(range(chips - half))]


def ring_pairs(device_count, shift):
    ring = chip_ring(device_count)
    size = len(ring)
    return [
        (2 * ring[k] + core, 2 * ring[(k + shift) % size] + core)
        for k in range(size)
        for core in range(2)
    ]


def send(value, pairs):
    return lax.ppermute(value, "expert", pairs)


def dp_shift(value, shift):
    count = lax.axis_size("dp")
    return lax.ppermute(value, "dp", [(p, (p + shift) % count) for p in range(count)])


def gather_planes(own):
    count = lax.axis_size("dp")
    return [own] + [dp_shift(own, -shift) for shift in range(1, count)]


def sum_planes(blocks):
    count = lax.axis_size("dp")
    total = blocks[0].astype(F32)
    for shift in range(1, count):
        total = total + dp_shift(blocks[shift], shift).astype(F32)
    return total.astype(BF16)


def flip_bit(device_count, bit):
    return [(i, i ^ bit) for i in range(device_count)]


def scatter_sum(blocks):
    count = blocks.shape[0]
    width = count.bit_length() - 1
    order = list(range(min(2, width))) + list(range(width - 1, 1, -1))
    index = lax.axis_index("expert")
    kept = list(range(width))
    shape = blocks.shape[1:]
    value = blocks.reshape((2,) * width + shape)
    for bit in order:
        axis = len(kept) - 1 - kept.index(bit)
        mine = (index >> bit) & 1
        keep = lax.dynamic_index_in_dim(value, mine, axis, keepdims=False)
        give = lax.dynamic_index_in_dim(value, 1 - mine, axis, keepdims=False)
        value = keep + send(give, flip_bit(count, 1 << bit))
        kept.remove(bit)
    return value


def ring_chain(value, sign, steps):
    count = lax.axis_size("expert")
    size = count // 2
    got = {}
    for step in range(1, steps + 1):
        value = send(value, ring_pairs(count, sign))
        got[-(size // 2) if 2 * step == size else -sign * step] = value
    return got


def ring_gather(value, far_right=True):
    size = lax.axis_size("expert") // 2
    far, near = size // 2, (size - 1) // 2
    got = {0: value}
    got.update(ring_chain(value, 1, far if far_right else near))
    got.update(ring_chain(value, -1, near if far_right else far))
    return got


def ring_order(count):
    size = count // 2
    distances = [0]
    for step in range(1, (size - 1) // 2 + 1):
        distances += [-step, step]
    return distances + ([-(size // 2)] if size % 2 == 0 else [])


def ring_sources(count):
    size = count // 2
    half = size // 2
    index = lax.axis_index("expert")
    chip = index // 2
    column = chip % 2
    place = jnp.where(column == 0, chip // 2, size - 1 - chip // 2)
    distances = jnp.array(ring_order(count) * 2, dtype=jnp.int32)
    other = jnp.array([0] * size + [1] * size, dtype=jnp.int32)
    there = lax.rem(place + distances + size, size)
    chip_there = jnp.where(there < half, 2 * there, 2 * (size - 1 - there) + 1)
    return 2 * chip_there + jnp.where(other == 1, 1 - index % 2, index % 2)


def grad_body(group, first, ids_ref, cols_ref, *refs):
    del ids_ref
    acts = refs[:group]
    dpres = refs[group : 2 * group]
    up_ref, down_ref = refs[2 * group + (0 if first else 2) :]
    step = pl.program_id(0)
    for k in range(group):

        @pl.when(step == k)
        def _(k=k):
            width = cols_ref.shape[2] // 2
            dims = (((0,), (0,)), ((), ()))
            up = lax.dot_general(
                cols_ref[0, :, :width], dpres[k][...], dims, preferred_element_type=F32
            )
            up_ref[0] = up.astype(BF16)
            down = lax.dot_general(
                cols_ref[0, :, width:], acts[k][...], dims, preferred_element_type=F32
            )
            down_ref[0] = down.astype(BF16)


def grad_stage(ids, cols, acts, dpres, totals, out_shape):
    group = len(acts)
    first = totals is None
    rows, hidden = acts[0].shape
    count, _, width = cols.shape
    block_rows = width // 2
    whole = pl.BlockSpec((rows, hidden), lambda i, ids: (0, 0))
    anywhere = pl.BlockSpec(memory_space=pl.ANY)
    out_spec = pl.BlockSpec((1, block_rows, hidden), lambda i, ids: (ids[i], 0, 0))
    return pl.pallas_call(
        functools.partial(grad_body, group, first),
        grid_spec=pltpu.PrefetchScalarGridSpec(
            num_scalar_prefetch=1,
            grid=(group,),
            in_specs=[pl.BlockSpec((1, rows, width), lambda i, ids: (ids[i], 0, 0))]
            + [whole] * (2 * group)
            + ([] if first else [anywhere, anywhere]),
            out_specs=[out_spec, out_spec],
        ),
        out_shape=[out_shape, out_shape],
        input_output_aliases={} if first else {2 + 2 * group: 0, 3 + 2 * group: 1},
        cost_estimate=pl.CostEstimate(
            flops=4 * group * rows * block_rows * hidden,
            bytes_accessed=4 * group * (rows + block_rows) * hidden,
            transcendentals=0,
        ),
        name="grad_stage",
    )(ids, cols, *acts, *dpres, *(() if first else totals))


def hot_body(ids_ref, cols_ref, act_ref, dpre_ref, up_in, down_in, up_ref, down_ref):
    del ids_ref
    width = cols_ref.shape[1] // 2
    dims = (((0,), (0,)), ((), ()))
    up = lax.dot_general(cols_ref[:, :width], dpre_ref[...], dims, preferred_element_type=F32)
    up_ref[0] = (up_in[0].astype(F32) + up).astype(BF16)
    down = lax.dot_general(cols_ref[:, width:], act_ref[...], dims, preferred_element_type=F32)
    down_ref[0] = (down_in[0].astype(F32) + down).astype(BF16)


def grad_hot(ids, cols, act, dpre, totals):
    rows, hidden = act.shape
    width = cols.shape[1]
    block_rows = width // 2
    whole = pl.BlockSpec((rows, hidden), lambda i, ids: (0, 0))
    spec = pl.BlockSpec((1, block_rows, hidden), lambda i, ids: (ids[0], 0, 0))
    out_shape = jax.ShapeDtypeStruct(totals[0].shape, BF16)
    return pl.pallas_call(
        hot_body,
        grid_spec=pltpu.PrefetchScalarGridSpec(
            num_scalar_prefetch=1,
            grid=(1,),
            in_specs=[pl.BlockSpec((rows, width), lambda i, ids: (0, 0)), whole, whole, spec, spec],
            out_specs=[spec, spec],
        ),
        out_shape=[out_shape, out_shape],
        input_output_aliases={4: 0, 5: 1},
        name="grad_hot",
    )(ids, cols, act, dpre, *totals)


def on_device(tokens, cotangent, gate_probs, expert_ids, route_slots, hot_mask, w_up, w_down):
    count = lax.axis_size("expert")
    planes = lax.axis_size("dp")
    index = lax.axis_index("expert")
    model_width = tokens.shape[1]
    up_local = w_up[0]
    down_local = w_down[0]
    hidden = up_local.shape[1]
    block_rows = model_width // count
    buffers = count * CAP
    swap = flip_bit(count, 1)
    codes = jnp.arange(count, dtype=jnp.int32)
    hot_index = jnp.sum(hot_mask * codes).astype(jnp.int32)
    is_owner = hot_index == index
    sources = ring_sources(count)
    order = ring_order(count)

    hot_extra = jnp.logical_and(expert_ids == hot_index, route_slots < HCAP)
    place = jnp.where(
        route_slots < CAP,
        expert_ids * CAP + route_slots,
        jnp.where(hot_extra, buffers + route_slots - CAP, -1),
    )
    slot_codes = jnp.arange(buffers + EXTRA, dtype=jnp.int32)
    picks = place[:, :, None] == slot_codes
    pick_first, pick_second = picks[:, 0].astype(BF16), picks[:, 1].astype(BF16)
    pick = pick_first + pick_second
    gate_rows = jnp.sum(jnp.where(picks, gate_probs[:, :, None], 0.0), axis=(0, 1))
    take = (((0,), (0,)), ((), ()))
    rows_x = lax.dot_general(pick, tokens, take, preferred_element_type=F32).astype(BF16)
    rows_g = (
        gate_rows[:, None] * lax.dot_general(pick, cotangent, take, preferred_element_type=F32)
    ).astype(BF16)

    def exchange(value):
        return lax.all_to_all(value, "expert", split_axis=0, concat_axis=0, tiled=True)

    extra = jnp.concatenate([rows_x[buffers:], rows_g[buffers:]], axis=1)
    extra = jnp.stack(gather_planes(extra), axis=0).reshape(-1, 2 * model_width)
    chain = ring_gather(extra)
    chain = jnp.concatenate([chain[d] for d in order])
    both_chains = jnp.concatenate([chain, send(chain, swap)]).reshape(
        2, count // 2, planes * EXTRA, 2 * model_width
    )

    rows = jnp.concatenate([rows_x[:buffers], rows_g[:buffers]], axis=1)
    arrived = exchange(rows.reshape(count, CAP, 2 * model_width))
    arrived_x, arrived_g = arrived[:, :, :model_width], arrived[:, :, model_width:]
    flat_x = jnp.concatenate(gather_planes(arrived_x)).reshape(-1, model_width)
    flat_g = jnp.concatenate(gather_planes(arrived_g)).reshape(-1, model_width)

    hot_rows_count = count * planes * EXTRA
    row_codes = jnp.arange(hot_rows_count, dtype=jnp.int32)
    row_sources = jnp.repeat(sources, planes * EXTRA) * (planes * EXTRA) + row_codes % (
        planes * EXTRA
    )
    sort_rows = jnp.logical_and(row_codes[:, None] == row_sources[None, :], is_owner).astype(BF16)
    flat_h = matmul(sort_rows, both_chains.reshape(hot_rows_count, -1)).astype(BF16)

    all_x = jnp.concatenate([flat_x, flat_h[:, :model_width]])
    all_g = jnp.concatenate([flat_g, flat_h[:, model_width:]])
    normal = flat_x.shape[0]
    gelu_value, gelu_slope = gelu_pair(matmul(all_x, up_local))
    activation = gelu_value.astype(BF16)
    act, hot_act = activation[:normal], activation[normal:]
    d_pre = (contract_last(all_g, down_local) * gelu_slope).astype(BF16)
    dpre, hot_dpre = d_pre[:normal], d_pre[normal:]

    acts = ring_gather(act)
    dpres = ring_gather(dpre, far_right=False)

    both = jnp.stack(
        [rows_x.reshape(-1, count, block_rows), rows_g.reshape(-1, count, block_rows)], axis=2
    )
    columns = exchange(jnp.transpose(both, (1, 0, 2, 3)).reshape(count, -1, 2 * block_rows))
    columns = jnp.stack(gather_planes(columns))
    cols = columns[:, :, :buffers].reshape(planes, count, count, CAP, 2 * block_rows)
    cols = jnp.transpose(cols, (2, 0, 1, 3, 4)).reshape(count, -1, 2 * block_rows)
    hot_cols = jnp.transpose(columns[:, :, buffers:], (1, 0, 2, 3)).reshape(-1, 2 * block_rows)

    part_out = matmul(activation, down_local).astype(BF16)
    part_back = contract_last(d_pre, up_local).astype(BF16)
    part = jnp.concatenate([part_out, part_back], axis=1)
    part_rows = part[:normal].reshape(planes, count, CAP, 2 * model_width)
    returned = exchange(sum_planes([part_rows[s] for s in range(planes)]))
    returned = returned.reshape(buffers, 2 * model_width)
    part_hot = part[normal:].reshape(count, planes, EXTRA, 2 * model_width)
    hot_back = sum_planes([part_hot[:, s] for s in range(planes)])
    hot_factors = jnp.concatenate([hot_act, hot_dpre], axis=1).reshape(count, -1, 2 * model_width)
    hot_rows = scatter_sum(jnp.concatenate([hot_back, hot_factors], axis=1))
    rows_back = jnp.concatenate([returned, hot_rows[:EXTRA]])
    back_out, back_grad = rows_back[:, :model_width], rows_back[:, model_width:]
    layer_out = (
        gate_probs[:, :1] * matmul(pick_first, back_out)
        + gate_probs[:, 1:] * matmul(pick_second, back_out)
    ).astype(BF16)
    grad_tokens = matmul(pick, back_grad).astype(BF16)

    out_shape = jax.ShapeDtypeStruct((count, block_rows, hidden), BF16)
    totals = None
    for start in range(0, len(order), 2):
        group = order[start : start + 2] if start else order[:2]
        mine_act, mine_dpre = [acts[d] for d in group], [dpres[d] for d in group]
        other_act = [send(v, swap) for v in mine_act]
        other_dpre = [send(v, swap) for v in mine_dpre]
        half = count // 2
        ids = jnp.concatenate(
            [sources[start : start + len(group)], sources[half + start : half + start + len(group)]]
        )
        totals = grad_stage(
            ids, cols, mine_act + other_act, mine_dpre + other_dpre, totals, out_shape
        )
    factors = hot_rows[EXTRA:]
    piece_rows = hot_rows_count // count
    chain = ring_gather(factors)
    chain = jnp.stack([chain[d] for d in order])
    hot_chains = jnp.concatenate([chain, send(chain, swap)]).reshape(-1, 2 * hidden)
    column_sources = jnp.repeat(sources, piece_rows) * piece_rows + row_codes % piece_rows
    sort_cols = (column_sources[:, None] == row_codes[None, :]).astype(BF16)
    hot_cols = matmul(sort_cols, hot_cols).astype(BF16)
    grad_up, grad_down = grad_hot(
        hot_index[None], hot_cols, hot_chains[:, :hidden], hot_chains[:, hidden:], totals
    )
    return (layer_out, grad_tokens, grad_up, grad_down)


def solution(mesh):
    placed = (
        P(("dp", "expert"), None),
        P(("dp", "expert"), None),
        P(("dp", "expert"), None),
        P(("dp", "expert"), None),
        P(("dp", "expert"), None),
        P(),
        P("expert", None, "dp"),
        P("expert", "dp", None),
    )
    return jax.shard_map(
        on_device,
        mesh=mesh,
        in_specs=placed,
        out_specs=(
            P(("dp", "expert"), None),
            P(("dp", "expert"), None),
            P(None, "expert", "dp"),
            P(None, "expert", "dp"),
        ),
        check_vma=False,
    )
```

```python
import functools

import jax
import jax.numpy as jnp
from jax import lax
from jax.experimental import pallas as pl
from jax.experimental.pallas import tpu as pltpu
from jax.sharding import PartitionSpec as P


CAP = 2
HCAP = 4
EXTRA = HCAP - CAP
BF16 = jnp.bfloat16
F32 = jnp.float32


def in_vmem(value):
    return pltpu.with_memory_space_constraint(value, pltpu.VMEM)


def in_hbm(value):
    return pltpu.with_memory_space_constraint(value, pltpu.HBM)


def gelu_pair(preact):
    normal_cdf = 0.5 * (1.0 + lax.erf(preact * 0.7071067811865476))
    density = jnp.exp(-0.5 * preact * preact) * 0.3989422804014327
    return (preact * normal_cdf, normal_cdf + preact * density)


def matmul(left, right):
    return jnp.dot(left, right, preferred_element_type=F32)


def chip_ring(device_count):
    chips = device_count // 2
    half = chips // 2
    return [2 * i for i in range(half)] + [2 * i + 1 for i in reversed(range(chips - half))]


def ring_pairs(device_count, shift):
    ring = chip_ring(device_count)
    size = len(ring)
    return [
        (2 * ring[k] + core, 2 * ring[(k + shift) % size] + core)
        for k in range(size)
        for core in range(2)
    ]


def send(value, pairs):
    return lax.ppermute(value, "expert", pairs)


def dp_shift(value, shift):
    count = lax.axis_size("dp")
    return lax.ppermute(value, "dp", [(p, (p + shift) % count) for p in range(count)])


def gather_planes(own):
    count = lax.axis_size("dp")
    return [own] + [dp_shift(own, -shift) for shift in range(1, count)]


def sum_planes(blocks):
    count = lax.axis_size("dp")
    total = blocks[0].astype(F32)
    for shift in range(1, count):
        total = total + dp_shift(blocks[shift], shift).astype(F32)
    return total.astype(BF16)


def flip_bit(device_count, bit):
    return [(i, i ^ bit) for i in range(device_count)]


def ring_gather(value):
    count = lax.axis_size("expert")
    size = count // 2
    right, left = ring_pairs(count, 1), ring_pairs(count, -1)
    got = {0: [value]}
    going_right = going_left = value
    for step in range(1, (size - 1) // 2 + 1):
        going_right = send(going_right, right)
        going_left = send(going_left, left)
        got[-step], got[step] = [going_right], [going_left]
    if size % 2 == 0:
        half = value.shape[0] // 2
        far_right = send(going_right[:half], right)
        far_left = send(going_left[half:], left)
        got[-(size // 2)] = [far_right, far_left]
    return got


def ring_groups(count):
    size = count // 2
    groups = [[0]] + [[-step, step] for step in range(1, (size - 1) // 2 + 1)]
    return groups + ([[-(size // 2)]] if size % 2 == 0 else [])


def ring_sources(count):
    size = count // 2
    half = size // 2
    index = lax.axis_index("expert")
    chip, core = index // 2, index % 2
    place = jnp.where(chip % 2 == 0, chip // 2, size - 1 - chip // 2)
    groups = ring_groups(count)
    distances = jnp.array([d for group in groups for d in group * 2], dtype=jnp.int32)
    other = jnp.array(
        [o for group in groups for o in [0] * len(group) + [1] * len(group)], dtype=jnp.int32
    )
    there = lax.rem(place + distances + size, size)
    chip_there = jnp.where(there < half, 2 * there, 2 * (size - 1 - there) + 1)
    return 2 * chip_there + jnp.where(other == 1, 1 - core, core)


def grad_body(layout, first, ids_ref, cols_ref, *refs):
    del ids_ref
    blocks = sum(layout)
    up_ref, down_ref = refs[blocks + (0 if first else 2) :]
    width = cols_ref.shape[2] // 2
    rows = cols_ref.shape[1]
    dims = (((0,), (0,)), ((), ()))
    step = pl.program_id(0)
    at = 0
    for k, parts in enumerate(layout):
        if parts == 1:
            act, dpre = refs[at].at[:rows], refs[at].at[rows:]
        else:
            act, dpre = refs[at], refs[at + 1]
        at += parts

        @pl.when(step == k)
        def _(act=act, dpre=dpre):
            up = lax.dot_general(
                cols_ref[0, :, :width], dpre[...], dims, preferred_element_type=F32
            )
            up_ref[0] = up.astype(BF16)
            down = lax.dot_general(
                cols_ref[0, :, width:], act[...], dims, preferred_element_type=F32
            )
            down_ref[0] = down.astype(BF16)


def grad_stage(ids, at, cols, chunks, totals, out_shape):
    group = len(chunks)
    first = totals is None
    layout = [len(chunk) for chunk in chunks]
    arrays = [block for chunk in chunks for block in chunk]
    _, rows, width = cols.shape
    hidden = arrays[0].shape[1]
    block_rows = width // 2
    anywhere = pl.BlockSpec(memory_space=pl.ANY)
    out_spec = pl.BlockSpec((1, block_rows, hidden), lambda i, ids: (ids[at + i], 0, 0))
    return pl.pallas_call(
        functools.partial(grad_body, layout, first),
        grid_spec=pltpu.PrefetchScalarGridSpec(
            num_scalar_prefetch=1,
            grid=(group,),
            in_specs=[pl.BlockSpec((1, rows, width), lambda i, ids: (ids[at + i], 0, 0))]
            + [pl.BlockSpec(memory_space=pltpu.VMEM)] * len(arrays)
            + ([] if first else [anywhere, anywhere]),
            out_specs=[out_spec, out_spec],
        ),
        out_shape=[out_shape, out_shape],
        input_output_aliases={} if first else {2 + len(arrays): 0, 3 + len(arrays): 1},
        cost_estimate=pl.CostEstimate(
            flops=4 * group * rows * block_rows * hidden,
            bytes_accessed=4 * group * (rows + block_rows) * hidden,
            transcendentals=0,
        ),
        compiler_params=pltpu.CompilerParams(vmem_limit_bytes=12 * 2**20),
        name="grad_stage",
    )(ids, cols, *[in_vmem(array) for array in arrays], *(() if first else totals))


def hot_body(ids_ref, cols_ref, rows_ref, up_in, down_in, up_ref, down_ref):
    del ids_ref
    width = cols_ref.shape[1] // 2
    dims = (((0,), (0,)), ((), ()))
    both = lax.dot_general(cols_ref[...], rows_ref[...], dims, preferred_element_type=F32)
    up_ref[0] = (up_in[0].astype(F32) + both[:width]).astype(BF16)
    down_ref[0] = (down_in[0].astype(F32) + both[width:]).astype(BF16)


def grad_hot(ids, cols, rows, totals):
    hidden = rows.shape[1]
    block_rows = cols.shape[1] // 2
    spec = pl.BlockSpec((1, block_rows, hidden), lambda i, ids: (ids[0], 0, 0))
    out_shape = jax.ShapeDtypeStruct(totals[0].shape, BF16)
    return pl.pallas_call(
        hot_body,
        grid_spec=pltpu.PrefetchScalarGridSpec(
            num_scalar_prefetch=1,
            grid=(1,),
            in_specs=[
                pl.BlockSpec(cols.shape, lambda i, ids: (0, 0)),
                pl.BlockSpec(rows.shape, lambda i, ids: (0, 0)),
                spec,
                spec,
            ],
            out_specs=[spec, spec],
        ),
        out_shape=[out_shape, out_shape],
        input_output_aliases={3: 0, 4: 1},
        compiler_params=pltpu.CompilerParams(vmem_limit_bytes=12 * 2**20),
        name="grad_hot",
    )(ids, cols, rows, *totals)


def ffn_body(
    normal, blocks, x_ref, g_ref, up_hbm, down_hbm, chunk_ref, hot_ref, up_ref, down_ref, pre, sems
):
    width, hidden = up_ref.shape
    rest = x_ref.shape[0] - normal
    rows, units = width // blocks, hidden // blocks
    ups = [pl.ds(k * rows, rows) for k in range(blocks)]
    downs = [pl.ds(k * units, units) for k in range(blocks)]
    copies = [
        pltpu.make_async_copy(up_hbm.at[here], up_ref.at[here], sems.at[0, k])
        for k, here in enumerate(ups)
    ] + [
        pltpu.make_async_copy(down_hbm.at[here], down_ref.at[here], sems.at[1, k])
        for k, here in enumerate(downs)
    ]
    for copy in copies:
        copy.start()
    for k, here in enumerate(ups):
        copies[k].wait()
        term = jnp.dot(x_ref[:, here], up_ref[here, :], preferred_element_type=F32)
        pre[...] = term if k == 0 else pre[...] + term
    for k, here in enumerate(downs):
        value, slope = gelu_pair(pre[:, here])
        value = value.astype(BF16)
        chunk_ref[:normal, here] = value[:normal]
        hot_ref[:rest, here] = value[normal:]
        copies[blocks + k].wait()
        d_act = lax.dot_general(
            g_ref[...], down_ref[here, :], (((1,), (1,)), ((), ())), preferred_element_type=F32
        )
        d_pre = (d_act * slope).astype(BF16)
        chunk_ref[normal:, here] = d_pre[:normal]
        hot_ref[rest:, here] = d_pre[normal:]


def ffn(normal, rows_in, rows_grad, up_local, down_local):
    total = rows_in.shape[0]
    width, hidden = up_local.shape
    blocks = 4
    vmem = pl.BlockSpec(memory_space=pltpu.VMEM)
    hbm = pl.BlockSpec(memory_space=pltpu.HBM)
    return pl.pallas_call(
        functools.partial(ffn_body, normal, blocks),
        in_specs=[vmem, vmem, hbm, hbm],
        out_specs=[vmem] * 4,
        out_shape=[
            jax.ShapeDtypeStruct((2 * normal, hidden), BF16),
            jax.ShapeDtypeStruct((2 * (total - normal), hidden), BF16),
            jax.ShapeDtypeStruct(up_local.shape, BF16),
            jax.ShapeDtypeStruct(down_local.shape, BF16),
        ],
        scratch_shapes=[
            pltpu.VMEM((total, hidden), F32),
            pltpu.SemaphoreType.DMA((2, blocks)),
        ],
        compiler_params=pltpu.CompilerParams(vmem_limit_bytes=12 * 2**20),
        cost_estimate=pl.CostEstimate(
            flops=4 * total * width * hidden,
            bytes_accessed=4 * width * hidden,
            transcendentals=2 * total * hidden,
        ),
        name="ffn",
    )(in_vmem(rows_in), in_vmem(rows_grad), in_hbm(up_local), in_hbm(down_local))


def parts_body(block, chunk_ref, hot_ref, up_ref, down_ref, part_ref, hot_part_ref, act, dpre):
    normal, rest = chunk_ref.shape[0] // 2, hot_ref.shape[0] // 2
    width = up_ref.shape[0]
    act[:normal], act[normal:] = chunk_ref[:normal], hot_ref[:rest]
    dpre[:normal], dpre[normal:] = chunk_ref[normal:], hot_ref[rest:]
    for at in range(0, width, block):
        here = pl.ds(at, block)
        out = jnp.dot(act[...], down_ref[:, here], preferred_element_type=F32).astype(BF16)
        part_ref[:, here], hot_part_ref[:, here] = out[:normal], out[normal:]
        back = lax.dot_general(
            dpre[...], up_ref[here, :], (((1,), (1,)), ((), ())), preferred_element_type=F32
        ).astype(BF16)
        there = pl.ds(width + at, block)
        part_ref[:, there], hot_part_ref[:, there] = back[:normal], back[normal:]


def parts(chunk, hot, up_local, down_local):
    width, hidden = up_local.shape
    normal, rest = chunk.shape[0] // 2, hot.shape[0] // 2
    vmem = pl.BlockSpec(memory_space=pltpu.VMEM)
    return pl.pallas_call(
        functools.partial(parts_body, 256),
        in_specs=[vmem] * 4,
        out_specs=[vmem, vmem],
        out_shape=[
            jax.ShapeDtypeStruct((normal, 2 * width), BF16),
            jax.ShapeDtypeStruct((rest, 2 * width), BF16),
        ],
        scratch_shapes=[pltpu.VMEM((normal + rest, hidden), BF16)] * 2,
        compiler_params=pltpu.CompilerParams(vmem_limit_bytes=12 * 2**20),
        cost_estimate=pl.CostEstimate(
            flops=4 * (normal + rest) * width * hidden,
            bytes_accessed=4 * width * hidden,
            transcendentals=0,
        ),
        name="parts",
    )(in_vmem(chunk), in_vmem(hot), in_vmem(up_local), in_vmem(down_local))


def on_device(tokens, cotangent, gate_probs, expert_ids, route_slots, hot_mask, w_up, w_down):
    count = lax.axis_size("expert")
    planes = lax.axis_size("dp")
    index = lax.axis_index("expert")
    model_width = tokens.shape[1]
    up_local = w_up[0]
    down_local = w_down[0]
    hidden = up_local.shape[1]
    block_rows = model_width // count
    buffers = count * CAP
    swap = flip_bit(count, 1)
    codes = jnp.arange(count, dtype=jnp.int32)
    hot_index = jnp.sum(hot_mask * codes).astype(jnp.int32)
    is_owner = hot_index == index
    sources = ring_sources(count)

    hot_extra = jnp.logical_and(expert_ids == hot_index, route_slots < HCAP)
    place = jnp.where(
        route_slots < CAP,
        expert_ids * CAP + route_slots,
        jnp.where(hot_extra, buffers + route_slots - CAP, -1),
    )
    slot_codes = jnp.arange(buffers + EXTRA, dtype=jnp.int32)
    picks = place[:, :, None] == slot_codes
    pick_first, pick_second = picks[:, 0].astype(BF16), picks[:, 1].astype(BF16)
    pick = pick_first + pick_second
    gate_rows = jnp.sum(jnp.where(picks, gate_probs[:, :, None], 0.0), axis=(0, 1))
    take = (((0,), (0,)), ((), ()))
    rows_x = lax.dot_general(pick, tokens, take, preferred_element_type=F32).astype(BF16)
    rows_g = (
        gate_rows[:, None] * lax.dot_general(pick, cotangent, take, preferred_element_type=F32)
    ).astype(BF16)

    def exchange(value):
        return lax.all_to_all(value, "expert", split_axis=0, concat_axis=0, tiled=True)

    def by_expert(values):
        extra = jnp.broadcast_to(values[None, buffers:], (count, EXTRA, model_width))
        return jnp.concatenate([values[:buffers].reshape(count, CAP, model_width), extra], axis=1)

    rows = jnp.concatenate([by_expert(rows_x), by_expert(rows_g)], axis=2)
    arrived = exchange(rows)
    arrived = jnp.stack(gather_planes(arrived))
    normal = planes * buffers
    flat = arrived[:, :, :CAP].reshape(-1, 2 * model_width)
    hot = arrived[:, :, CAP:].reshape(-1, 2 * model_width)
    flat = jnp.concatenate([flat, jnp.where(is_owner, hot, jnp.zeros_like(hot))])
    chunk, hot_factors, up_held, down_held = ffn(
        normal, flat[:, :model_width], flat[:, model_width:], up_local, down_local
    )
    hot_rows_count = hot_factors.shape[0] // 2

    chunks = ring_gather(chunk)

    def by_column_block(values):
        return values.reshape(-1, count, block_rows)

    both = jnp.concatenate(
        [by_column_block(rows_x[:buffers]), by_column_block(rows_g[:buffers])], axis=2
    )
    columns = exchange(jnp.transpose(both, (1, 0, 2)))
    columns = gather_planes(columns)
    cols = jnp.stack(columns).reshape(planes, count, count, CAP, 2 * block_rows)
    cols = jnp.transpose(cols, (2, 0, 1, 3, 4)).reshape(count, -1, 2 * block_rows)

    part, part_hot = parts(chunk, hot_factors, up_held, down_held)
    part_rows = part.reshape(planes, count, CAP, 2 * model_width)
    part_hot = part_hot.reshape(planes, count, EXTRA, 2 * model_width)
    part_rows = [
        jnp.concatenate([part_rows[s], part_hot[s]], axis=1) for s in range(planes)
    ]
    summed = sum_planes(part_rows)
    pieces = hot_factors.reshape(count, -1, 2 * model_width)
    returned = exchange(jnp.concatenate([summed, pieces], axis=1))
    hot_back = lax.dynamic_index_in_dim(returned[:, CAP:], hot_index, 0, keepdims=False)
    hot_back, piece = hot_back[:EXTRA], hot_back[EXTRA:]
    rows_back = jnp.concatenate(
        [returned[:, :CAP].reshape(buffers, 2 * model_width), hot_back]
    )
    back_out, back_grad = rows_back[:, :model_width], rows_back[:, model_width:]
    layer_out = (
        gate_probs[:, :1] * matmul(pick_first, back_out)
        + gate_probs[:, 1:] * matmul(pick_second, back_out)
    ).astype(BF16)
    grad_tokens = matmul(pick, back_grad).astype(BF16)

    out_shape = jax.ShapeDtypeStruct((count, block_rows, hidden), BF16)
    totals = None
    at = 0
    groups = ring_groups(count)
    for group in groups:
        mine = [chunks[d] for d in group]
        others = [[send(block, swap) for block in chunk] for chunk in mine]
        totals = grad_stage(sources, at, cols, mine + others, totals, out_shape)
        at += 2 * len(group)

    piece = piece.reshape(1, -1, hidden)
    hot_rows = exchange(jnp.broadcast_to(piece, (count,) + piece.shape[1:]))
    hot_rows = hot_rows.reshape(-1, hidden)
    hot_x, hot_g = [
        lax.dynamic_slice_in_dim(hot, half * model_width + index * block_rows, block_rows, 1)
        for half in range(2)
    ]
    none = jnp.zeros((hot_rows_count, block_rows), BF16)
    table = jnp.concatenate(
        [jnp.concatenate([none, hot_g], axis=1), jnp.concatenate([hot_x, none], axis=1)]
    )
    grad_up, grad_down = grad_hot(hot_index[None], table, hot_rows, totals)
    return (layer_out, grad_tokens, grad_up, grad_down)


def solution(mesh):
    placed = (
        P(("dp", "expert"), None),
        P(("dp", "expert"), None),
        P(("dp", "expert"), None),
        P(("dp", "expert"), None),
        P(("dp", "expert"), None),
        P(),
        P("expert", None, "dp"),
        P("expert", "dp", None),
    )

    return jax.shard_map(
        on_device,
        mesh=mesh,
        in_specs=placed,
        out_specs=(
            P(("dp", "expert"), None),
            P(("dp", "expert"), None),
            P(None, "expert", "dp"),
            P(None, "expert", "dp"),
        ),
        check_vma=False,
    )
```

```python
import functools

import jax
import jax.numpy as jnp
from jax import lax
from jax.experimental import pallas as pl
from jax.experimental.pallas import tpu as pltpu
from jax.sharding import PartitionSpec as P


CAP = 2
HCAP = 4
EXTRA = HCAP - CAP
BF16 = jnp.bfloat16
F32 = jnp.float32


def in_vmem(value):
    return pltpu.with_memory_space_constraint(value, pltpu.VMEM)


def in_hbm(value):
    return pltpu.with_memory_space_constraint(value, pltpu.HBM)


def gelu_pair(preact):
    normal_cdf = 0.5 * (1.0 + lax.erf(preact * 0.7071067811865476))
    density = jnp.exp(-0.5 * preact * preact) * 0.3989422804014327
    return (preact * normal_cdf, normal_cdf + preact * density)


def matmul(left, right):
    return jnp.dot(left, right, preferred_element_type=F32)


def chip_ring(device_count):
    chips = device_count // 2
    half = chips // 2
    return [2 * i for i in range(half)] + [2 * i + 1 for i in reversed(range(chips - half))]


def ring_pairs(device_count, shift):
    ring = chip_ring(device_count)
    size = len(ring)
    return [
        (2 * ring[k] + core, 2 * ring[(k + shift) % size] + core)
        for k in range(size)
        for core in range(2)
    ]


def send(value, pairs):
    return lax.ppermute(value, "expert", pairs)


def dp_shift(value, shift):
    count = lax.axis_size("dp")
    return lax.ppermute(value, "dp", [(p, (p + shift) % count) for p in range(count)])


def gather_planes(own):
    count = lax.axis_size("dp")
    return [own] + [dp_shift(own, -shift) for shift in range(1, count)]


def flip_bit(device_count, bit):
    return [(i, i ^ bit) for i in range(device_count)]


def ring_gather(value, split_far=True):
    count = lax.axis_size("expert")
    size = count // 2
    right, left = ring_pairs(count, 1), ring_pairs(count, -1)
    got = {0: [value]}
    going_right = going_left = value
    for step in range(1, (size - 1) // 2 + 1):
        going_right = send(going_right, right)
        going_left = send(going_left, left)
        got[-step], got[step] = [going_right], [going_left]
    if size % 2 == 0 and not split_far:
        got[-(size // 2)] = [send(going_right, right)]
    elif size % 2 == 0:
        half = value.shape[0] // 2
        far_right = send(going_right[:half], right)
        far_left = send(going_left[half:], left)
        got[-(size // 2)] = [far_right, far_left]
    return got


def ring_groups(count):
    size = count // 2
    groups = [[0]] + [[-step, step] for step in range(1, (size - 1) // 2 + 1)]
    return groups + ([[-(size // 2)]] if size % 2 == 0 else [])


def ring_sources(count):
    size = count // 2
    half = size // 2
    index = lax.axis_index("expert")
    chip, core = index // 2, index % 2
    place = jnp.where(chip % 2 == 0, chip // 2, size - 1 - chip // 2)
    groups = ring_groups(count)
    distances = jnp.array([d for group in groups for d in group * 2], dtype=jnp.int32)
    other = jnp.array(
        [o for group in groups for o in [0] * len(group) + [1] * len(group)], dtype=jnp.int32
    )
    there = lax.rem(place + distances + size, size)
    chip_there = jnp.where(there < half, 2 * there, 2 * (size - 1 - there) + 1)
    return 2 * chip_there + jnp.where(other == 1, 1 - core, core)


def grad_body(layout, first, ids_ref, cols_ref, *refs):
    del ids_ref
    blocks = sum(layout)
    up_ref, down_ref = refs[blocks + (0 if first else 2) :]
    width = cols_ref.shape[2] // 2
    rows = cols_ref.shape[1]
    dims = (((0,), (0,)), ((), ()))
    step = pl.program_id(0)
    at = 0
    for k, parts in enumerate(layout):
        if parts == 1:
            act, dpre = refs[at].at[:rows], refs[at].at[rows:]
        else:
            act, dpre = refs[at], refs[at + 1]
        at += parts

        @pl.when(step == k)
        def _(act=act, dpre=dpre):
            up = lax.dot_general(
                cols_ref[0, :, :width], dpre[...], dims, preferred_element_type=F32
            )
            up_ref[0] = up.astype(BF16)
            down = lax.dot_general(
                cols_ref[0, :, width:], act[...], dims, preferred_element_type=F32
            )
            down_ref[0] = down.astype(BF16)


def grad_stage(ids, at, cols, chunks, totals, out_shape):
    group = len(chunks)
    first = totals is None
    layout = [len(chunk) for chunk in chunks]
    arrays = [block for chunk in chunks for block in chunk]
    _, rows, width = cols.shape
    hidden = arrays[0].shape[1]
    block_rows = width // 2
    anywhere = pl.BlockSpec(memory_space=pl.ANY)
    out_spec = pl.BlockSpec((1, block_rows, hidden), lambda i, ids: (ids[at + i], 0, 0))
    return pl.pallas_call(
        functools.partial(grad_body, layout, first),
        grid_spec=pltpu.PrefetchScalarGridSpec(
            num_scalar_prefetch=1,
            grid=(group,),
            in_specs=[pl.BlockSpec((1, rows, width), lambda i, ids: (ids[at + i], 0, 0))]
            + [pl.BlockSpec(memory_space=pltpu.VMEM)] * len(arrays)
            + ([] if first else [anywhere, anywhere]),
            out_specs=[out_spec, out_spec],
        ),
        out_shape=[out_shape, out_shape],
        input_output_aliases={} if first else {2 + len(arrays): 0, 3 + len(arrays): 1},
        cost_estimate=pl.CostEstimate(
            flops=4 * group * rows * block_rows * hidden,
            bytes_accessed=4 * group * (rows + block_rows) * hidden,
            transcendentals=0,
        ),
        compiler_params=pltpu.CompilerParams(vmem_limit_bytes=12 * 2**20),
        name="grad_stage",
    )(ids, cols, *[in_vmem(array) for array in arrays], *(() if first else totals))


def last_body(
    group, at, ids_ref, cols_ref, table_ref, rows_ref, *refs
):
    acts, dpres = refs[0 : 2 * group : 2], refs[1 : 2 * group : 2]
    up_in, down_in, up_out, down_out = refs[2 * group : 2 * group + 4]
    held, both, sems = refs[2 * group + 4 :]
    del up_in, down_in
    hot = ids_ref[ids_ref.shape[0] - 1]
    block_rows = held.shape[2]
    dims = (((0,), (0,)), ((), ()))
    outs = (up_out, down_out)
    ours = [ids_ref[at + k] for k in range(group)]
    elsewhere = functools.reduce(jnp.logical_and, [expert != hot for expert in ours])

    def moves(slot, expert, into):
        pairs = [(held.at[slot, side], outs[side].at[expert]) for side in range(2)]
        pairs = [(b, a) for a, b in pairs] if into else pairs
        return [
            pltpu.make_async_copy(a, b, sems.at[slot, side]) for side, (a, b) in enumerate(pairs)
        ]

    @pl.when(elsewhere)
    def _():
        for copy in moves(group, hot, True):
            copy.start()

    both[...] = lax.dot_general(
        table_ref[...], rows_ref[...], dims, preferred_element_type=F32
    )
    for k in range(group):
        cols = cols_ref[ours[k]]
        mine = jnp.where(ours[k] == hot, 1.0, 0.0)
        for side, factor in ((0, dpres[k]), (1, acts[k])):
            value = lax.dot_general(
                cols[:, side * block_rows : (side + 1) * block_rows],
                factor[...],
                dims,
                preferred_element_type=F32,
            )
            value += mine * both[side * block_rows : (side + 1) * block_rows]
            held[k, side] = value.astype(BF16)
        for copy in moves(k, ours[k], False):
            copy.start()

    @pl.when(elsewhere)
    def _():
        for copy in moves(group, hot, True):
            copy.wait()
        for side in range(2):
            value = held[group, side].astype(F32)
            value += both[side * block_rows : (side + 1) * block_rows]
            held[group, side] = value.astype(BF16)
        for copy in moves(group, hot, False):
            copy.start()
        for copy in moves(group, hot, False):
            copy.wait()

    for k in range(group):
        for copy in moves(k, ours[k], False):
            copy.wait()


def last_stage(ids, at, hot_index, cols, table, rows, chunks, totals):
    group = len(chunks)
    arrays = [block for chunk in chunks for block in chunk]
    hidden = rows.shape[1]
    block_rows = table.shape[1] // 2
    out_shape = jax.ShapeDtypeStruct(totals[0].shape, BF16)
    vmem = pl.BlockSpec(memory_space=pltpu.VMEM)
    hbm = pl.BlockSpec(memory_space=pltpu.HBM)
    return pl.pallas_call(
        functools.partial(last_body, group, at),
        in_specs=[pl.BlockSpec(memory_space=pltpu.SMEM)]
        + [vmem] * (3 + len(arrays))
        + [hbm, hbm],
        out_specs=[hbm, hbm],
        out_shape=[out_shape, out_shape],
        scratch_shapes=[
            pltpu.VMEM((group + 1, 2, block_rows, hidden), BF16),
            pltpu.VMEM((2 * block_rows, hidden), F32),
            pltpu.SemaphoreType.DMA((group + 1, 2)),
        ],
        input_output_aliases={4 + len(arrays): 0, 5 + len(arrays): 1},
        compiler_params=pltpu.CompilerParams(vmem_limit_bytes=16 * 2**20),
        cost_estimate=pl.CostEstimate(
            flops=8 * group * table.size * hidden,
            bytes_accessed=8 * group * block_rows * hidden,
            transcendentals=0,
        ),
        name="last_stage",
    )(
        jnp.concatenate([ids, hot_index[None]]),
        cols,
        table,
        rows,
        *[in_vmem(array) for array in arrays],
        *totals,
    )


def load_body(up_hbm, down_hbm, up_ref, down_ref, sems):
    copies = [
        pltpu.make_async_copy(up_hbm, up_ref, sems.at[0]),
        pltpu.make_async_copy(down_hbm, down_ref, sems.at[1]),
    ]
    for copy in copies:
        copy.start()
    for copy in copies:
        copy.wait()


def load(up_local, down_local):
    hbm, vmem = pl.BlockSpec(memory_space=pltpu.HBM), pl.BlockSpec(memory_space=pltpu.VMEM)
    return pl.pallas_call(
        load_body,
        in_specs=[hbm, hbm],
        out_specs=[vmem, vmem],
        out_shape=[
            jax.ShapeDtypeStruct(weights.shape, BF16) for weights in (up_local, down_local)
        ],
        scratch_shapes=[pltpu.SemaphoreType.DMA((2,))],
        compiler_params=pltpu.CompilerParams(vmem_limit_bytes=2**20),
        cost_estimate=pl.CostEstimate(
            flops=0, bytes_accessed=8 * up_local.size, transcendentals=0
        ),
        name="load",
    )(in_hbm(up_local), in_hbm(down_local))


def pick_rows(count, rows, want):
    have = lax.broadcasted_iota(jnp.int32, (count, rows), 1)
    return jnp.where(have == want, 1.0, 0.0).astype(BF16)


def ffn_body(planes, block, owner_ref, *refs):
    arrived = refs[:planes]
    up_ref, down_ref, chunk_ref, hot_ref, x_ref, g_ref = refs[planes:]
    rows = arrived[0].shape[0]
    mine = rows // (2 * HCAP) * CAP
    extra = rows // (2 * HCAP) * EXTRA
    normal, rest = planes * mine, planes * extra
    hidden = up_ref.shape[1]
    at = lax.broadcasted_iota(jnp.int32, (normal + rest, 1), 0)
    hot_at = at - normal
    is_hot = at >= normal
    plane = jnp.where(is_hot, hot_at // extra, at // mine)
    within = jnp.where(is_hot, hot_at % extra, at % mine)
    line = jnp.where(
        is_hot,
        within // EXTRA * (2 * HCAP) + CAP + within % EXTRA,
        within // CAP * (2 * HCAP) + within % CAP,
    )
    line = jnp.where(jnp.logical_and(is_hot, owner_ref[0] == 0), -2 * HCAP, line)
    for to_ref, shift in ((x_ref, 0), (g_ref, HCAP)):
        value = None
        for s in range(planes):
            pick = pick_rows(normal + rest, rows, jnp.where(plane == s, line + shift, -1))
            term = jnp.dot(pick, arrived[s][...], preferred_element_type=F32)
            value = term if value is None else value + term
        to_ref[...] = value.astype(BF16)
    for at in range(0, hidden, block):
        here = pl.ds(at, block)
        preact = jnp.dot(x_ref[...], up_ref[:, here], preferred_element_type=F32)
        value, slope = gelu_pair(preact)
        value = value.astype(BF16)
        chunk_ref[:normal, here] = value[:normal]
        hot_ref[:rest, here] = value[normal:]
        d_act = lax.dot_general(
            g_ref[...], down_ref[here, :], (((1,), (1,)), ((), ())), preferred_element_type=F32
        )
        d_pre = (d_act * slope).astype(BF16)
        chunk_ref[normal:, here] = d_pre[:normal]
        hot_ref[rest:, here] = d_pre[normal:]


def ffn(owner, arrived, up_held, down_held):
    planes = len(arrived)
    width, hidden = up_held.shape
    blocks = arrived[0].shape[0] // (2 * HCAP)
    normal, rest = planes * blocks * CAP, planes * blocks * EXTRA
    vmem = pl.BlockSpec(memory_space=pltpu.VMEM)
    return pl.pallas_call(
        functools.partial(ffn_body, planes, min(hidden, 256)),
        in_specs=[pl.BlockSpec(memory_space=pltpu.SMEM)] + [vmem] * (planes + 2),
        out_specs=[vmem, vmem],
        out_shape=[
            jax.ShapeDtypeStruct((2 * normal, hidden), BF16),
            jax.ShapeDtypeStruct((2 * rest, hidden), BF16),
        ],
        scratch_shapes=[pltpu.VMEM((normal + rest, width), BF16)] * 2,
        compiler_params=pltpu.CompilerParams(
            vmem_limit_bytes=12 * 2**20 + 16 * (normal + rest) * width
        ),
        cost_estimate=pl.CostEstimate(
            flops=4 * (normal + rest) * width * hidden,
            bytes_accessed=4 * width * hidden,
            transcendentals=2 * (normal + rest) * hidden,
        ),
        name="ffn",
    )(owner, *arrived, in_vmem(up_held), in_vmem(down_held))


def parts_body(block, chunk_ref, hot_ref, up_ref, down_ref, part_ref, act, dpre):
    normal, rest = chunk_ref.shape[0] // 2, hot_ref.shape[0] // 2
    planes = part_ref.shape[0]
    width = up_ref.shape[0]
    act[:normal], act[normal:] = chunk_ref[:normal], hot_ref[:rest]
    dpre[:normal], dpre[normal:] = chunk_ref[normal:], hot_ref[rest:]
    mine, extra = normal // planes, rest // planes

    def put(rows, here):
        for s in range(planes):
            part_ref[s, :mine, here] = rows[s * mine : (s + 1) * mine]
            part_ref[s, mine:, here] = rows[normal + s * extra : normal + (s + 1) * extra]

    for at in range(0, width, block):
        here = pl.ds(at, block)
        out = jnp.dot(act[...], down_ref[:, here], preferred_element_type=F32).astype(BF16)
        put(out, here)
        back = lax.dot_general(
            dpre[...], up_ref[here, :], (((1,), (1,)), ((), ())), preferred_element_type=F32
        ).astype(BF16)
        put(back, pl.ds(width + at, block))


def parts(planes, chunk, hot, up_local, down_local):
    width, hidden = up_local.shape
    rows = (chunk.shape[0] + hot.shape[0]) // 2
    vmem = pl.BlockSpec(memory_space=pltpu.VMEM)
    return pl.pallas_call(
        functools.partial(parts_body, 256),
        in_specs=[vmem] * 4,
        out_specs=vmem,
        out_shape=jax.ShapeDtypeStruct((planes, rows // planes, 2 * width), BF16),
        scratch_shapes=[pltpu.VMEM((rows, hidden), BF16)] * 2,
        compiler_params=pltpu.CompilerParams(vmem_limit_bytes=12 * 2**20),
        cost_estimate=pl.CostEstimate(
            flops=4 * rows * width * hidden,
            bytes_accessed=4 * width * hidden,
            transcendentals=0,
        ),
        name="parts",
    )(in_vmem(chunk), in_vmem(hot), in_vmem(up_local), in_vmem(down_local))


def back_body(count, piece_rows, piece_ref, *refs):
    parts_in, out_ref = refs[:-1], refs[-1]
    rows = parts_in[0].shape[0]
    width = out_ref.shape[1]
    slots = 2 * HCAP + piece_rows
    total = count * slots
    at = lax.broadcasted_iota(jnp.int32, (total, 1), 0)
    place, line = at // slots, at % slots
    within = line % HCAP
    row = jnp.where(
        within < CAP, place * CAP + within, count * CAP + place * EXTRA + within - CAP
    )
    outs = pick_rows(total, rows, jnp.where(line < HCAP, row, -1))
    backs = pick_rows(
        total, rows, jnp.where(jnp.logical_and(line >= HCAP, line < 2 * HCAP), row, -1)
    )
    pieces = pick_rows(total, piece_rows, line - 2 * HCAP)

    def summed(here):
        value = parts_in[0][:, here].astype(F32)
        for part in parts_in[1:]:
            value = value + part[:, here].astype(F32)
        return value.astype(BF16)

    block = 512
    for start in range(0, width, block):
        here, there = pl.ds(start, block), pl.ds(width + start, block)
        value = jnp.dot(outs, summed(here), preferred_element_type=F32)
        value += jnp.dot(backs, summed(there), preferred_element_type=F32)
        value += jnp.dot(pieces, piece_ref[:, here], preferred_element_type=F32)
        out_ref[:, here] = value.astype(BF16)


def back_rows(count, piece, parts_in):
    piece_rows, width = piece.shape
    slots = 2 * HCAP + piece_rows
    vmem = pl.BlockSpec(memory_space=pltpu.VMEM)
    return pl.pallas_call(
        functools.partial(back_body, count, piece_rows),
        in_specs=[vmem] * (1 + len(parts_in)),
        out_specs=vmem,
        out_shape=jax.ShapeDtypeStruct((count * slots, width), BF16),
        compiler_params=pltpu.CompilerParams(vmem_limit_bytes=24 * 2**20),
        cost_estimate=pl.CostEstimate(
            flops=8 * count * slots * parts_in[0].shape[0] * width,
            bytes_accessed=2 * count * slots * width,
            transcendentals=0,
        ),
        name="back_rows",
    )(piece, *parts_in).reshape(count, slots, width)


def combine_body(codes_ref, gates_ref, rows_ref, out_ref, back_ref):
    tokens, rows = out_ref.shape[0], rows_ref.shape[0]
    have = lax.broadcasted_iota(jnp.int32, (rows, tokens), 0)

    def pick(want):
        return jnp.where(have == want, 1.0, 0.0).astype(BF16)

    picks = [pick(codes_ref[c : c + 1, :]) for c in range(2)]
    back = pick(codes_ref[0:1, :] + HCAP) + pick(codes_ref[1:2, :] + HCAP)
    gates = jnp.transpose(gates_ref[...])
    take = (((0,), (0,)), ((), ()))
    width = out_ref.shape[1]
    block = 512
    for start in range(0, width, block):
        here = pl.ds(start, block)
        value = [
            lax.dot_general(pick, rows_ref[:, here], take, preferred_element_type=F32)
            for pick in picks
        ]
        out_ref[:, here] = (gates[:, 0:1] * value[0] + gates[:, 1:2] * value[1]).astype(BF16)
        back_ref[:, here] = lax.dot_general(
            back, rows_ref[:, here], take, preferred_element_type=F32
        ).astype(BF16)


def combine(codes, gates, rows):
    shape = jax.ShapeDtypeStruct((codes.shape[0], rows.shape[1]), BF16)
    vmem = pl.BlockSpec(memory_space=pltpu.VMEM)
    return pl.pallas_call(
        combine_body,
        in_specs=[vmem] * 3,
        out_specs=[vmem] * 2,
        out_shape=[shape, shape],
        compiler_params=pltpu.CompilerParams(vmem_limit_bytes=16 * 2**20),
        cost_estimate=pl.CostEstimate(
            flops=6 * rows.size * codes.shape[0], bytes_accessed=6 * rows.size, transcendentals=0
        ),
        name="combine",
    )(jnp.pad(codes.T, ((0, 6), (0, 0))), jnp.pad(gates.T, ((0, 6), (0, 0))), rows)


def pack_body(mask_ref, *refs):
    from_refs, (out_ref, normal_ref), (*to_refs, sems) = refs[:5], refs[5:7], refs[7:]
    copies = [
        pltpu.make_async_copy(a, b, sems.at[k]) for k, (a, b) in enumerate(zip(from_refs, to_refs))
    ]
    for copy in copies:
        copy.start()
    for copy in copies:
        copy.wait()
    ids_ref, slots_ref, gates_ref, tokens_ref, grad_ref = to_refs
    hot_index = 0
    for e in range(mask_ref.shape[0]):
        hot_index = jnp.where(mask_ref[e] > 0, e, hot_index)
    ids, route_slots = ids_ref[...], slots_ref[...]
    kept = route_slots < CAP
    normal_codes = jnp.where(kept, ids * CAP + route_slots, -2)
    extra = jnp.logical_and(ids == hot_index, jnp.logical_not(kept))
    hot_codes = jnp.where(extra, route_slots, -2)
    rows, tokens = out_ref.shape[0], tokens_ref.shape[0]
    at = lax.broadcasted_iota(jnp.int32, (rows, 1), 0)
    slots = 2 * HCAP
    line = at % slots
    within = line % HCAP
    normal = jnp.where(within < CAP, at // slots * CAP + within, -1)
    hot = jnp.where(within < CAP, -1, within)
    picks = jnp.zeros((rows, tokens), F32)
    gates = jnp.zeros((rows, 1), F32)
    count = normal_ref.shape[1]
    normal_at = lax.broadcasted_iota(jnp.int32, (count, 1), 0)
    normal_picks = jnp.zeros((count, tokens), F32)
    normal_gates = jnp.zeros((count, 1), F32)
    for c in range(2):
        gate = gates_ref[c : c + 1, :]
        to_normal, to_hot = normal_codes[c : c + 1, :], hot_codes[c : c + 1, :]
        pick = jnp.logical_or(to_normal == normal, to_hot == hot)
        picks += jnp.where(pick, 1.0, 0.0)
        gates += jnp.sum(jnp.where(pick, gate, 0.0), axis=1, keepdims=True)
        pick = to_normal == normal_at
        normal_picks += jnp.where(pick, 1.0, 0.0)
        normal_gates += jnp.sum(jnp.where(pick, gate, 0.0), axis=1, keepdims=True)
    picks_x = jnp.where(line < HCAP, picks, 0.0).astype(BF16)
    picks_g = jnp.where(line < HCAP, 0.0, picks).astype(BF16)
    normal_picks = normal_picks.astype(BF16)
    width = out_ref.shape[1]
    block = 512
    for start in range(0, width, block):
        here = pl.ds(start, block)
        x, g = tokens_ref[:, here], grad_ref[:, here]
        value = jnp.dot(picks_x, x, preferred_element_type=F32)
        value += gates * jnp.dot(picks_g, g, preferred_element_type=F32)
        out_ref[:, here] = value.astype(BF16)
        normal_ref[0, :, here] = jnp.dot(normal_picks, x, preferred_element_type=F32).astype(BF16)
        normal_ref[1, :, here] = (
            normal_gates * jnp.dot(normal_picks, g, preferred_element_type=F32)
        ).astype(BF16)


def pack(count, mask, ids, route_slots, gates, tokens, cotangent):
    width = tokens.shape[1]
    vmem = pl.BlockSpec(memory_space=pltpu.VMEM)
    slots = 2 * HCAP
    rows = count * (slots + 2 * CAP)
    arrays = (ids, route_slots, gates, tokens, cotangent)
    return pl.pallas_call(
        pack_body,
        in_specs=[pl.BlockSpec(memory_space=pltpu.SMEM)]
        + [pl.BlockSpec(memory_space=pltpu.HBM)] * 5,
        out_specs=[vmem] * 2,
        out_shape=[
            jax.ShapeDtypeStruct((count * slots, width), BF16),
            jax.ShapeDtypeStruct((2, count * CAP, width), BF16),
        ],
        scratch_shapes=[pltpu.VMEM(array.shape, array.dtype) for array in arrays]
        + [pltpu.SemaphoreType.DMA((len(arrays),))],
        compiler_params=pltpu.CompilerParams(vmem_limit_bytes=16 * 2**20),
        cost_estimate=pl.CostEstimate(
            flops=4 * rows * tokens.size, bytes_accessed=2 * rows * width, transcendentals=0
        ),
        name="pack",
    )(mask, *[in_hbm(array) for array in arrays])


def on_device(tokens, cotangent, gate_probs, expert_ids, route_slots, hot_mask, w_up, w_down):
    count = lax.axis_size("expert")
    planes = lax.axis_size("dp")
    index = lax.axis_index("expert")
    model_width = tokens.shape[1]
    up_local = w_up[0]
    down_local = w_down[0]
    hidden = up_local.shape[1]
    block_rows = model_width // count
    buffers = count * CAP
    swap = flip_bit(count, 1)
    codes = jnp.arange(count, dtype=jnp.int32)
    hot_index = jnp.sum(hot_mask * codes).astype(jnp.int32)
    owner = (hot_index == index).astype(jnp.int32)[None]
    sources = ring_sources(count)

    hot_extra = jnp.logical_and(
        expert_ids == hot_index, jnp.logical_and(route_slots >= CAP, route_slots < HCAP)
    )
    kept_normal = route_slots < CAP
    rows, normal_rows = pack(
        count, hot_mask, expert_ids.T, route_slots.T, gate_probs.T, tokens, cotangent
    )

    def exchange(value):
        return lax.all_to_all(value, "expert", split_axis=0, concat_axis=0, tiled=True)

    slots = 2 * HCAP
    arrived = exchange(rows.reshape(count, slots, model_width))
    arrived = gather_planes(arrived.reshape(count * slots, model_width))
    up_held, down_held = load(up_local, down_local)
    chunk, hot_factors = ffn(
        owner, arrived, up_held, down_held
    )
    hot_rows_count = hot_factors.shape[0] // 2

    chunks = ring_gather(chunk)

    part = parts(planes, chunk, hot_factors, up_held, down_held)
    part, *arrived = lax.optimization_barrier((part, *arrived))

    both = normal_rows.reshape(2, buffers, count, block_rows)
    both = jnp.transpose(jnp.concatenate([both[0], both[1]], axis=2), (1, 0, 2))
    columns = exchange(both)
    part, columns = lax.optimization_barrier((part, columns))
    columns = gather_planes(columns)
    place = jnp.arange(count * buffers, dtype=jnp.int32)
    turned = (place // CAP % count * count + place // buffers) * CAP + place % CAP
    turn = (turned[:, None] == place[None, :]).astype(BF16)
    cols = jnp.concatenate(
        [
            matmul(turn, block.reshape(count * buffers, 2 * block_rows))
            .astype(BF16)
            .reshape(count, buffers, 2 * block_rows)
            for block in columns
        ],
        axis=1,
    )

    received = [part[0]] + [dp_shift(part[s], s) for s in range(1, planes)]
    pieces = exchange(hot_factors.reshape(count, -1, model_width))
    piece = lax.dynamic_index_in_dim(pieces, hot_index, 0, keepdims=False)
    returned = back_rows(count, piece, received)
    returned = exchange(returned)
    back_slots = returned.shape[1]
    came = jnp.where(
        jnp.logical_or(kept_normal, hot_extra), expert_ids * back_slots + route_slots, -HCAP - 1
    )
    layer_out, grad_tokens = combine(
        came, gate_probs, returned.reshape(count * back_slots, model_width)
    )

    out_shape = jax.ShapeDtypeStruct((count, block_rows, hidden), BF16)
    totals = None
    at = 0
    groups = ring_groups(count)
    for k, group in enumerate(groups):
        mine = [chunks[d] for d in group]
        others = [[send(block, swap) for block in chunk] for chunk in mine]
        if k + 1 == len(groups):
            break
        totals = grad_stage(sources, at, cols, mine + others, totals, out_shape)
        at += 2 * len(group)

    hot_rows = returned[:, 2 * HCAP :].reshape(-1, hidden)
    held = jnp.concatenate(
        [
            lax.dynamic_slice_in_dim(block, index * block_rows, block_rows, 1)
            for block in arrived
        ]
    )
    hot_at = jnp.arange(hot_rows_count, dtype=jnp.int32)
    line = hot_at // EXTRA * slots + CAP + hot_at % EXTRA
    line_codes = jnp.arange(planes * count * slots, dtype=jnp.int32)
    none = jnp.full((hot_rows_count,), -1, jnp.int32)

    def pick_columns(want):
        return matmul((want[:, None] == line_codes[None, :]).astype(BF16), held).astype(BF16)

    table = jnp.concatenate(
        [
            pick_columns(jnp.concatenate([none, line])),
            pick_columns(jnp.concatenate([line + HCAP, none])),
        ],
        axis=1,
    )
    grad_up, grad_down = last_stage(
        sources, at, hot_index, cols, table, hot_rows, mine + others, totals
    )
    return (layer_out, grad_tokens, grad_up, grad_down)


def solution(mesh):
    placed = (
        P(("dp", "expert"), None),
        P(("dp", "expert"), None),
        P(("dp", "expert"), None),
        P(("dp", "expert"), None),
        P(("dp", "expert"), None),
        P(),
        P("expert", None, "dp"),
        P("expert", "dp", None),
    )

    return jax.shard_map(
        on_device,
        mesh=mesh,
        in_specs=placed,
        out_specs=(
            P(("dp", "expert"), None),
            P(("dp", "expert"), None),
            P(None, "expert", "dp"),
            P(None, "expert", "dp"),
        ),
        check_vma=False,
    )
```

```python
import functools

import jax
import jax.numpy as jnp
from jax import lax
from jax.experimental import pallas as pl
from jax.experimental.pallas import tpu as pltpu
from jax.sharding import PartitionSpec as P


CAP = 2
HCAP = 4
EXTRA = HCAP - CAP
BF16 = jnp.bfloat16
F32 = jnp.float32


def in_vmem(value):
    return pltpu.with_memory_space_constraint(value, pltpu.VMEM)


def in_hbm(value):
    return pltpu.with_memory_space_constraint(value, pltpu.HBM)


def gelu_pair(preact):
    normal_cdf = 0.5 * (1.0 + lax.erf(preact * 0.7071067811865476))
    density = jnp.exp(-0.5 * preact * preact) * 0.3989422804014327
    return (preact * normal_cdf, normal_cdf + preact * density)


def matmul(left, right):
    return jnp.dot(left, right, preferred_element_type=F32)


def chip_ring(device_count):
    chips = device_count // 2
    half = chips // 2
    return [2 * i for i in range(half)] + [2 * i + 1 for i in reversed(range(chips - half))]


def ring_pairs(device_count, shift):
    ring = chip_ring(device_count)
    size = len(ring)
    return [
        (2 * ring[k] + core, 2 * ring[(k + shift) % size] + core)
        for k in range(size)
        for core in range(2)
    ]


def send(value, pairs):
    return lax.ppermute(value, "expert", pairs)


def dp_shift(value, shift):
    count = lax.axis_size("dp")
    return lax.ppermute(value, "dp", [(p, (p + shift) % count) for p in range(count)])


def gather_planes(own):
    count = lax.axis_size("dp")
    return [own] + [dp_shift(own, -shift) for shift in range(1, count)]


def flip_bit(device_count, bit):
    return [(i, i ^ bit) for i in range(device_count)]


def ring_gather(value, split_far=True):
    count = lax.axis_size("expert")
    size = count // 2
    right, left = ring_pairs(count, 1), ring_pairs(count, -1)
    got = {0: [value]}
    going_right = going_left = value
    for step in range(1, (size - 1) // 2 + 1):
        going_right = send(going_right, right)
        going_left = send(going_left, left)
        got[-step], got[step] = [going_right], [going_left]
    if size % 2 == 0 and not split_far:
        got[-(size // 2)] = [send(going_right, right)]
    elif size % 2 == 0:
        half = value.shape[0] // 2
        far_right = send(going_right[:half], right)
        far_left = send(going_left[half:], left)
        got[-(size // 2)] = [far_right, far_left]
    return got


def ring_groups(count):
    size = count // 2
    groups = [[0]] + [[-step, step] for step in range(1, (size - 1) // 2 + 1)]
    return groups + ([[-(size // 2)]] if size % 2 == 0 else [])


def ring_sources(count):
    size = count // 2
    half = size // 2
    index = lax.axis_index("expert")
    chip, core = index // 2, index % 2
    place = jnp.where(chip % 2 == 0, chip // 2, size - 1 - chip // 2)
    groups = ring_groups(count)
    distances = jnp.array([d for group in groups for d in group * 2], dtype=jnp.int32)
    other = jnp.array(
        [o for group in groups for o in [0] * len(group) + [1] * len(group)], dtype=jnp.int32
    )
    there = lax.rem(place + distances + size, size)
    chip_there = jnp.where(there < half, 2 * there, 2 * (size - 1 - there) + 1)
    return 2 * chip_there + jnp.where(other == 1, 1 - core, core)


def grad_body(layout, first, ids_ref, cols_ref, *refs):
    del ids_ref
    blocks = sum(layout)
    up_ref, down_ref = refs[blocks + (0 if first else 2) :]
    width = cols_ref.shape[2] // 2
    rows = cols_ref.shape[1]
    dims = (((0,), (0,)), ((), ()))
    step = pl.program_id(0)
    at = 0
    for k, parts in enumerate(layout):
        if parts == 1:
            act, dpre = refs[at].at[:rows], refs[at].at[rows:]
        else:
            act, dpre = refs[at], refs[at + 1]
        at += parts

        @pl.when(step == k)
        def _(act=act, dpre=dpre):
            up = lax.dot_general(
                cols_ref[0, :, :width], dpre[...], dims, preferred_element_type=F32
            )
            up_ref[0] = up.astype(BF16)
            down = lax.dot_general(
                cols_ref[0, :, width:], act[...], dims, preferred_element_type=F32
            )
            down_ref[0] = down.astype(BF16)


def grad_stage(ids, at, cols, chunks, totals, out_shape):
    group = len(chunks)
    first = totals is None
    layout = [len(chunk) for chunk in chunks]
    arrays = [block for chunk in chunks for block in chunk]
    _, rows, width = cols.shape
    hidden = arrays[0].shape[1]
    block_rows = width // 2
    anywhere = pl.BlockSpec(memory_space=pl.ANY)
    out_spec = pl.BlockSpec((1, block_rows, hidden), lambda i, ids: (ids[at + i], 0, 0))
    return pl.pallas_call(
        functools.partial(grad_body, layout, first),
        grid_spec=pltpu.PrefetchScalarGridSpec(
            num_scalar_prefetch=1,
            grid=(group,),
            in_specs=[pl.BlockSpec((1, rows, width), lambda i, ids: (ids[at + i], 0, 0))]
            + [pl.BlockSpec(memory_space=pltpu.VMEM)] * len(arrays)
            + ([] if first else [anywhere, anywhere]),
            out_specs=[out_spec, out_spec],
        ),
        out_shape=[out_shape, out_shape],
        input_output_aliases={} if first else {2 + len(arrays): 0, 3 + len(arrays): 1},
        cost_estimate=pl.CostEstimate(
            flops=4 * group * rows * block_rows * hidden,
            bytes_accessed=4 * group * (rows + block_rows) * hidden,
            transcendentals=0,
        ),
        compiler_params=pltpu.CompilerParams(vmem_limit_bytes=12 * 2**20),
        name="grad_stage",
    )(ids, cols, *[in_vmem(array) for array in arrays], *(() if first else totals))


def last_body(
    group, at, ids_ref, cols_ref, table_ref, rows_ref, *refs
):
    acts, dpres = refs[0 : 2 * group : 2], refs[1 : 2 * group : 2]
    up_in, down_in, up_out, down_out = refs[2 * group : 2 * group + 4]
    held, both, sems = refs[2 * group + 4 :]
    del up_in, down_in
    hot = ids_ref[ids_ref.shape[0] - 1]
    block_rows = held.shape[2]
    dims = (((0,), (0,)), ((), ()))
    outs = (up_out, down_out)
    ours = [ids_ref[at + k] for k in range(group)]
    elsewhere = functools.reduce(jnp.logical_and, [expert != hot for expert in ours])

    def moves(slot, expert, into):
        pairs = [(held.at[slot, side], outs[side].at[expert]) for side in range(2)]
        pairs = [(b, a) for a, b in pairs] if into else pairs
        return [
            pltpu.make_async_copy(a, b, sems.at[slot, side]) for side, (a, b) in enumerate(pairs)
        ]

    @pl.when(elsewhere)
    def _():
        for copy in moves(group, hot, True):
            copy.start()

    both[...] = lax.dot_general(
        table_ref[...], rows_ref[...], dims, preferred_element_type=F32
    )
    for k in range(group):
        cols = cols_ref[ours[k]]
        mine = jnp.where(ours[k] == hot, 1.0, 0.0)
        for side, factor in ((0, dpres[k]), (1, acts[k])):
            value = lax.dot_general(
                cols[:, side * block_rows : (side + 1) * block_rows],
                factor[...],
                dims,
                preferred_element_type=F32,
            )
            value += mine * both[side * block_rows : (side + 1) * block_rows]
            held[k, side] = value.astype(BF16)
        for copy in moves(k, ours[k], False):
            copy.start()

    @pl.when(elsewhere)
    def _():
        for copy in moves(group, hot, True):
            copy.wait()
        for side in range(2):
            value = held[group, side].astype(F32)
            value += both[side * block_rows : (side + 1) * block_rows]
            held[group, side] = value.astype(BF16)
        for copy in moves(group, hot, False):
            copy.start()
        for copy in moves(group, hot, False):
            copy.wait()

    for k in range(group):
        for copy in moves(k, ours[k], False):
            copy.wait()


def last_stage(ids, at, cols, table, rows, chunks, totals):
    group = len(chunks)
    arrays = [block for chunk in chunks for block in chunk]
    hidden = rows.shape[1]
    block_rows = table.shape[1] // 2
    out_shape = jax.ShapeDtypeStruct(totals[0].shape, BF16)
    vmem = pl.BlockSpec(memory_space=pltpu.VMEM)
    hbm = pl.BlockSpec(memory_space=pltpu.HBM)
    return pl.pallas_call(
        functools.partial(last_body, group, at),
        in_specs=[pl.BlockSpec(memory_space=pltpu.SMEM)]
        + [vmem] * (3 + len(arrays))
        + [hbm, hbm],
        out_specs=[hbm, hbm],
        out_shape=[out_shape, out_shape],
        scratch_shapes=[
            pltpu.VMEM((group + 1, 2, block_rows, hidden), BF16),
            pltpu.VMEM((2 * block_rows, hidden), F32),
            pltpu.SemaphoreType.DMA((group + 1, 2)),
        ],
        input_output_aliases={4 + len(arrays): 0, 5 + len(arrays): 1},
        compiler_params=pltpu.CompilerParams(vmem_limit_bytes=16 * 2**20),
        cost_estimate=pl.CostEstimate(
            flops=8 * group * table.size * hidden,
            bytes_accessed=8 * group * block_rows * hidden,
            transcendentals=0,
        ),
        name="last_stage",
    )(
        ids,
        cols,
        table,
        rows,
        *[in_vmem(array) for array in arrays],
        *totals,
    )


def load_body(up_hbm, down_hbm, up_ref, down_ref, sems):
    copies = [
        pltpu.make_async_copy(up_hbm, up_ref, sems.at[0]),
        pltpu.make_async_copy(down_hbm, down_ref, sems.at[1]),
    ]
    for copy in copies:
        copy.start()
    for copy in copies:
        copy.wait()


def load(up_local, down_local):
    hbm, vmem = pl.BlockSpec(memory_space=pltpu.HBM), pl.BlockSpec(memory_space=pltpu.VMEM)
    return pl.pallas_call(
        load_body,
        in_specs=[hbm, hbm],
        out_specs=[vmem, vmem],
        out_shape=[
            jax.ShapeDtypeStruct(weights.shape, BF16) for weights in (up_local, down_local)
        ],
        scratch_shapes=[pltpu.SemaphoreType.DMA((2,))],
        compiler_params=pltpu.CompilerParams(vmem_limit_bytes=2**20),
        cost_estimate=pl.CostEstimate(
            flops=0, bytes_accessed=8 * up_local.size, transcendentals=0
        ),
        name="load",
    )(in_hbm(up_local), in_hbm(down_local))


def pick_rows(count, rows, want):
    have = lax.broadcasted_iota(jnp.int32, (count, rows), 1)
    return jnp.where(have == want, 1.0, 0.0).astype(BF16)


def ffn_body(planes, block, owner_ref, *refs):
    arrived = refs[:planes]
    up_ref, down_ref, chunk_ref, hot_ref, x_ref, g_ref = refs[planes:]
    rows = arrived[0].shape[0]
    mine = rows // (2 * HCAP) * CAP
    extra = rows // (2 * HCAP) * EXTRA
    normal, rest = planes * mine, planes * extra
    hidden = up_ref.shape[1]
    at = lax.broadcasted_iota(jnp.int32, (normal + rest, 1), 0)
    hot_at = at - normal
    is_hot = at >= normal
    plane = jnp.where(is_hot, hot_at // extra, at // mine)
    within = jnp.where(is_hot, hot_at % extra, at % mine)
    line = jnp.where(
        is_hot,
        within // EXTRA * (2 * HCAP) + CAP + within % EXTRA,
        within // CAP * (2 * HCAP) + within % CAP,
    )
    line = jnp.where(jnp.logical_and(is_hot, owner_ref[0] == 0), -2 * HCAP, line)
    for to_ref, shift in ((x_ref, 0), (g_ref, HCAP)):
        value = None
        for s in range(planes):
            pick = pick_rows(normal + rest, rows, jnp.where(plane == s, line + shift, -1))
            term = jnp.dot(pick, arrived[s][...], preferred_element_type=F32)
            value = term if value is None else value + term
        to_ref[...] = value.astype(BF16)
    for at in range(0, hidden, block):
        here = pl.ds(at, block)
        preact = jnp.dot(x_ref[...], up_ref[:, here], preferred_element_type=F32)
        value, slope = gelu_pair(preact)
        value = value.astype(BF16)
        chunk_ref[:normal, here] = value[:normal]
        hot_ref[:rest, here] = value[normal:]
        d_act = lax.dot_general(
            g_ref[...], down_ref[here, :], (((1,), (1,)), ((), ())), preferred_element_type=F32
        )
        d_pre = (d_act * slope).astype(BF16)
        chunk_ref[normal:, here] = d_pre[:normal]
        hot_ref[rest:, here] = d_pre[normal:]


def ffn(owner, arrived, up_held, down_held):
    planes = len(arrived)
    width, hidden = up_held.shape
    blocks = arrived[0].shape[0] // (2 * HCAP)
    normal, rest = planes * blocks * CAP, planes * blocks * EXTRA
    vmem = pl.BlockSpec(memory_space=pltpu.VMEM)
    return pl.pallas_call(
        functools.partial(ffn_body, planes, min(hidden, 256)),
        in_specs=[pl.BlockSpec(memory_space=pltpu.SMEM)] + [vmem] * (planes + 2),
        out_specs=[vmem, vmem],
        out_shape=[
            jax.ShapeDtypeStruct((2 * normal, hidden), BF16),
            jax.ShapeDtypeStruct((2 * rest, hidden), BF16),
        ],
        scratch_shapes=[pltpu.VMEM((normal + rest, width), BF16)] * 2,
        compiler_params=pltpu.CompilerParams(
            vmem_limit_bytes=12 * 2**20 + 16 * (normal + rest) * width
        ),
        cost_estimate=pl.CostEstimate(
            flops=4 * (normal + rest) * width * hidden,
            bytes_accessed=4 * width * hidden,
            transcendentals=2 * (normal + rest) * hidden,
        ),
        name="ffn",
    )(owner, *arrived, in_vmem(up_held), in_vmem(down_held))


def parts_body(block, chunk_ref, hot_ref, up_ref, down_ref, part_ref, act, dpre):
    normal, rest = chunk_ref.shape[0] // 2, hot_ref.shape[0] // 2
    planes = part_ref.shape[0]
    width = up_ref.shape[0]
    act[:normal], act[normal:] = chunk_ref[:normal], hot_ref[:rest]
    dpre[:normal], dpre[normal:] = chunk_ref[normal:], hot_ref[rest:]
    mine, extra = normal // planes, rest // planes

    def put(rows, here):
        for s in range(planes):
            part_ref[s, :mine, here] = rows[s * mine : (s + 1) * mine]
            part_ref[s, mine:, here] = rows[normal + s * extra : normal + (s + 1) * extra]

    for at in range(0, width, block):
        here = pl.ds(at, block)
        out = jnp.dot(act[...], down_ref[:, here], preferred_element_type=F32).astype(BF16)
        put(out, here)
        back = lax.dot_general(
            dpre[...], up_ref[here, :], (((1,), (1,)), ((), ())), preferred_element_type=F32
        ).astype(BF16)
        put(back, pl.ds(width + at, block))


def parts(planes, chunk, hot, up_local, down_local):
    width, hidden = up_local.shape
    rows = (chunk.shape[0] + hot.shape[0]) // 2
    vmem = pl.BlockSpec(memory_space=pltpu.VMEM)
    return pl.pallas_call(
        functools.partial(parts_body, 256),
        in_specs=[vmem] * 4,
        out_specs=vmem,
        out_shape=jax.ShapeDtypeStruct((planes, rows // planes, 2 * width), BF16),
        scratch_shapes=[pltpu.VMEM((rows, hidden), BF16)] * 2,
        compiler_params=pltpu.CompilerParams(vmem_limit_bytes=12 * 2**20),
        cost_estimate=pl.CostEstimate(
            flops=4 * rows * width * hidden,
            bytes_accessed=4 * width * hidden,
            transcendentals=0,
        ),
        name="parts",
    )(in_vmem(chunk), in_vmem(hot), in_vmem(up_local), in_vmem(down_local))


def back_body(count, piece_ref, *refs):
    parts_in, out_ref = refs[:-1], refs[-1]
    rows = parts_in[0].shape[0]
    width = out_ref.shape[2]
    slots = 2 * HCAP
    total = count * slots
    at = lax.broadcasted_iota(jnp.int32, (total, 1), 0)
    place, line = at // slots, at % slots
    within = line % HCAP
    row = jnp.where(
        within < CAP, place * CAP + within, count * CAP + place * EXTRA + within - CAP
    )
    outs = pick_rows(total, rows, jnp.where(line < HCAP, row, -1))
    backs = pick_rows(total, rows, jnp.where(line < HCAP, -1, row))
    for k in range(count):
        out_ref[k, slots:] = piece_ref[...]

    def summed(here):
        value = parts_in[0][:, here].astype(F32)
        for part in parts_in[1:]:
            value = value + part[:, here].astype(F32)
        return value.astype(BF16)

    block = 512
    for start in range(0, width, block):
        here, there = pl.ds(start, block), pl.ds(width + start, block)
        value = jnp.dot(outs, summed(here), preferred_element_type=F32)
        value += jnp.dot(backs, summed(there), preferred_element_type=F32)
        value = value.astype(BF16)
        for k in range(count):
            out_ref[k, :slots, here] = value[k * slots : (k + 1) * slots]


def back_rows(count, piece, parts_in):
    piece_rows, width = piece.shape
    slots = 2 * HCAP + piece_rows
    vmem = pl.BlockSpec(memory_space=pltpu.VMEM)
    return pl.pallas_call(
        functools.partial(back_body, count),
        in_specs=[vmem] * (1 + len(parts_in)),
        out_specs=vmem,
        out_shape=jax.ShapeDtypeStruct((count, slots, width), BF16),
        compiler_params=pltpu.CompilerParams(vmem_limit_bytes=24 * 2**20),
        cost_estimate=pl.CostEstimate(
            flops=8 * count * slots * parts_in[0].shape[0] * width,
            bytes_accessed=2 * count * slots * width,
            transcendentals=0,
        ),
        name="back_rows",
    )(piece, *parts_in)


def combine_body(codes_ref, gates_ref, rows_ref, out_ref, back_ref):
    tokens, rows = out_ref.shape[0], rows_ref.shape[0]
    have = lax.broadcasted_iota(jnp.int32, (rows, tokens), 0)

    def pick(want):
        return jnp.where(have == want, 1.0, 0.0).astype(BF16)

    picks = [pick(codes_ref[c : c + 1, :]) for c in range(2)]
    back = pick(codes_ref[0:1, :] + HCAP) + pick(codes_ref[1:2, :] + HCAP)
    gates = jnp.transpose(gates_ref[...])
    take = (((0,), (0,)), ((), ()))
    width = out_ref.shape[1]
    block = 512
    for start in range(0, width, block):
        here = pl.ds(start, block)
        value = [
            lax.dot_general(pick, rows_ref[:, here], take, preferred_element_type=F32)
            for pick in picks
        ]
        out_ref[:, here] = (gates[:, 0:1] * value[0] + gates[:, 1:2] * value[1]).astype(BF16)
        back_ref[:, here] = lax.dot_general(
            back, rows_ref[:, here], take, preferred_element_type=F32
        ).astype(BF16)


def combine(codes, gates, rows):
    shape = jax.ShapeDtypeStruct((codes.shape[0], rows.shape[1]), BF16)
    vmem = pl.BlockSpec(memory_space=pltpu.VMEM)
    return pl.pallas_call(
        combine_body,
        in_specs=[vmem] * 3,
        out_specs=[vmem] * 2,
        out_shape=[shape, shape],
        compiler_params=pltpu.CompilerParams(vmem_limit_bytes=16 * 2**20),
        cost_estimate=pl.CostEstimate(
            flops=6 * rows.size * codes.shape[0], bytes_accessed=6 * rows.size, transcendentals=0
        ),
        name="combine",
    )(jnp.pad(codes.T, ((0, 6), (0, 0))), jnp.pad(gates.T, ((0, 6), (0, 0))), rows)


def pack_body(mask_ref, *refs):
    from_refs, (out_ref, normal_ref), (*to_refs, sems) = refs[:5], refs[5:7], refs[7:]
    copies = [
        pltpu.make_async_copy(a, b, sems.at[k]) for k, (a, b) in enumerate(zip(from_refs, to_refs))
    ]
    for copy in copies:
        copy.start()
    for copy in copies:
        copy.wait()
    ids_ref, slots_ref, gates_ref, tokens_ref, grad_ref = to_refs
    hot_index = 0
    for e in range(mask_ref.shape[0]):
        hot_index = jnp.where(mask_ref[e] > 0, e, hot_index)
    ids, route_slots = ids_ref[...], slots_ref[...]
    kept = route_slots < CAP
    normal_codes = jnp.where(kept, ids * CAP + route_slots, -2)
    extra = jnp.logical_and(ids == hot_index, jnp.logical_not(kept))
    hot_codes = jnp.where(extra, route_slots, -2)
    rows, tokens = out_ref.shape[0], tokens_ref.shape[0]
    at = lax.broadcasted_iota(jnp.int32, (rows, 1), 0)
    slots = 2 * HCAP
    line = at % slots
    within = line % HCAP
    normal = jnp.where(within < CAP, at // slots * CAP + within, -1)
    hot = jnp.where(within < CAP, -1, within)
    picks = jnp.zeros((rows, tokens), F32)
    gates = jnp.zeros((rows, 1), F32)
    count = normal_ref.shape[1]
    normal_at = lax.broadcasted_iota(jnp.int32, (count, 1), 0)
    normal_picks = jnp.zeros((count, tokens), F32)
    normal_gates = jnp.zeros((count, 1), F32)
    for c in range(2):
        gate = gates_ref[c : c + 1, :]
        to_normal, to_hot = normal_codes[c : c + 1, :], hot_codes[c : c + 1, :]
        pick = jnp.logical_or(to_normal == normal, to_hot == hot)
        picks += jnp.where(pick, 1.0, 0.0)
        gates += jnp.sum(jnp.where(pick, gate, 0.0), axis=1, keepdims=True)
        pick = to_normal == normal_at
        normal_picks += jnp.where(pick, 1.0, 0.0)
        normal_gates += jnp.sum(jnp.where(pick, gate, 0.0), axis=1, keepdims=True)
    picks_x = jnp.where(line < HCAP, picks, 0.0).astype(BF16)
    picks_g = jnp.where(line < HCAP, 0.0, picks).astype(BF16)
    normal_picks = normal_picks.astype(BF16)
    width = out_ref.shape[1]
    block = 512
    for start in range(0, width, block):
        here = pl.ds(start, block)
        x, g = tokens_ref[:, here], grad_ref[:, here]
        value = jnp.dot(picks_x, x, preferred_element_type=F32)
        value += gates * jnp.dot(picks_g, g, preferred_element_type=F32)
        out_ref[:, here] = value.astype(BF16)
        normal_ref[0, :, here] = jnp.dot(normal_picks, x, preferred_element_type=F32).astype(BF16)
        normal_ref[1, :, here] = (
            normal_gates * jnp.dot(normal_picks, g, preferred_element_type=F32)
        ).astype(BF16)


def pack(count, mask, ids, route_slots, gates, tokens, cotangent):
    width = tokens.shape[1]
    vmem = pl.BlockSpec(memory_space=pltpu.VMEM)
    slots = 2 * HCAP
    rows = count * (slots + 2 * CAP)
    arrays = (ids, route_slots, gates, tokens, cotangent)
    return pl.pallas_call(
        pack_body,
        in_specs=[pl.BlockSpec(memory_space=pltpu.SMEM)]
        + [pl.BlockSpec(memory_space=pltpu.HBM)] * 5,
        out_specs=[vmem] * 2,
        out_shape=[
            jax.ShapeDtypeStruct((count * slots, width), BF16),
            jax.ShapeDtypeStruct((2, count * CAP, width), BF16),
        ],
        scratch_shapes=[pltpu.VMEM(array.shape, array.dtype) for array in arrays]
        + [pltpu.SemaphoreType.DMA((len(arrays),))],
        compiler_params=pltpu.CompilerParams(vmem_limit_bytes=16 * 2**20),
        cost_estimate=pl.CostEstimate(
            flops=4 * rows * tokens.size, bytes_accessed=2 * rows * width, transcendentals=0
        ),
        name="pack",
    )(mask, *[in_hbm(array) for array in arrays])


def on_device(tokens, cotangent, gate_probs, expert_ids, route_slots, hot_mask, w_up, w_down):
    count = lax.axis_size("expert")
    planes = lax.axis_size("dp")
    index = lax.axis_index("expert")
    model_width = tokens.shape[1]
    up_local = w_up[0]
    down_local = w_down[0]
    hidden = up_local.shape[1]
    block_rows = model_width // count
    buffers = count * CAP
    swap = flip_bit(count, 1)
    codes = jnp.arange(count, dtype=jnp.int32)
    hot_index = jnp.sum(hot_mask * codes).astype(jnp.int32)
    owner = (hot_index == index).astype(jnp.int32)[None]
    sources = ring_sources(count)
    last_ids = jnp.concatenate([sources, hot_index[None]])

    hot_extra = jnp.logical_and(
        expert_ids == hot_index, jnp.logical_and(route_slots >= CAP, route_slots < HCAP)
    )
    kept_normal = route_slots < CAP
    rows, normal_rows = pack(
        count, hot_mask, expert_ids.T, route_slots.T, gate_probs.T, tokens, cotangent
    )

    def exchange(value):
        return lax.all_to_all(value, "expert", split_axis=0, concat_axis=0, tiled=True)

    slots = 2 * HCAP
    arrived = exchange(rows.reshape(count, slots, model_width))
    arrived = gather_planes(arrived.reshape(count * slots, model_width))
    up_held, down_held = load(up_local, down_local)
    chunk, hot_factors = ffn(
        owner, arrived, up_held, down_held
    )
    hot_rows_count = hot_factors.shape[0] // 2

    chunks = ring_gather(chunk)

    part = parts(planes, chunk, hot_factors, up_held, down_held)
    part, *arrived = lax.optimization_barrier((part, *arrived))

    both = normal_rows.reshape(2, buffers, count, block_rows)
    both = jnp.transpose(jnp.concatenate([both[0], both[1]], axis=2), (1, 0, 2))
    columns = exchange(both)
    part, columns = lax.optimization_barrier((part, columns))
    columns = gather_planes(columns)
    place = jnp.arange(count * buffers, dtype=jnp.int32)
    turned = (place // CAP % count * count + place // buffers) * CAP + place % CAP
    turn = (turned[:, None] == place[None, :]).astype(BF16)
    cols = jnp.concatenate(
        [
            matmul(turn, block.reshape(count * buffers, 2 * block_rows))
            .astype(BF16)
            .reshape(count, buffers, 2 * block_rows)
            for block in columns
        ],
        axis=1,
    )

    received = [part[0]] + [dp_shift(part[s], s) for s in range(1, planes)]
    pieces = exchange(hot_factors.reshape(count, -1, model_width))
    piece = lax.dynamic_index_in_dim(pieces, hot_index, 0, keepdims=False)
    returned = back_rows(count, piece, received)
    returned = exchange(returned)
    back_slots = returned.shape[1]
    came = jnp.where(
        jnp.logical_or(kept_normal, hot_extra), expert_ids * back_slots + route_slots, -HCAP - 1
    )
    layer_out, grad_tokens = combine(
        came, gate_probs, returned.reshape(count * back_slots, model_width)
    )

    out_shape = jax.ShapeDtypeStruct((count, block_rows, hidden), BF16)
    totals = None
    at = 0
    groups = ring_groups(count)
    for k, group in enumerate(groups):
        mine = [chunks[d] for d in group]
        others = [[send(block, swap) for block in chunk] for chunk in mine]
        if k + 1 == len(groups):
            break
        totals = grad_stage(sources, at, cols, mine + others, totals, out_shape)
        at += 2 * len(group)

    hot_rows = returned[:, 2 * HCAP :].reshape(-1, hidden)
    held = jnp.concatenate(
        [
            lax.dynamic_slice_in_dim(block, index * block_rows, block_rows, 1)
            for block in arrived
        ]
    )
    hot_at = jnp.arange(hot_rows_count, dtype=jnp.int32)
    line = hot_at // EXTRA * slots + CAP + hot_at % EXTRA
    line_codes = jnp.arange(planes * count * slots, dtype=jnp.int32)
    none = jnp.full((hot_rows_count,), -1, jnp.int32)

    def pick_columns(want):
        return matmul((want[:, None] == line_codes[None, :]).astype(BF16), held).astype(BF16)

    table = jnp.concatenate(
        [
            pick_columns(jnp.concatenate([none, line])),
            pick_columns(jnp.concatenate([line + HCAP, none])),
        ],
        axis=1,
    )
    grad_up, grad_down = last_stage(
        last_ids, at, cols, table, hot_rows, mine + others, totals
    )
    return (layer_out, grad_tokens, grad_up, grad_down)


def solution(mesh):
    placed = (
        P(("dp", "expert"), None),
        P(("dp", "expert"), None),
        P(("dp", "expert"), None),
        P(("dp", "expert"), None),
        P(("dp", "expert"), None),
        P(),
        P("expert", None, "dp"),
        P("expert", "dp", None),
    )

    return jax.shard_map(
        on_device,
        mesh=mesh,
        in_specs=placed,
        out_specs=(
            P(("dp", "expert"), None),
            P(("dp", "expert"), None),
            P(None, "expert", "dp"),
            P(None, "expert", "dp"),
        ),
        check_vma=False,
    )
```
